512 devices in a mesh: gx: 32 (over z, x), gy: 16 (over y, core).
Axes of the slice: x: 4, y: 8, z: 8, core: 2. Of those that a mesh axis runs over, the one named last changes fastest.
Arguments:
- velocity_guess: float32 [8, 2, 1024, 4096], P(None, None, 'gx', 'gy'), may hold values from -6 to 6
- friction: bfloat16 [8, 1024, 4096], P(None, 'gx', 'gy'), may hold values from 0.5 to 4
- thickness: float32 [1024, 4096], P('gx', 'gy'), may hold values from 0.5 to 4.5
- surface: float32 [1024, 4096], P('gx', 'gy'), may hold values from -4 to 1284
- ice_mask: int32 [1024, 4096], P('gx', 'gy'), may hold values 0 or 1
- grounded_mask: int32 [1024, 4096], P('gx', 'gy'), may hold values 0 or 1
Outputs:
- velocity: float32 [8, 2, 1024, 4096], P(None, None, 'gx', 'gy')
The draws below stay inside these ranges and needn't reach their ends.
All inputs are finite; a program needn't handle non-finite values. No bound on the sum of `ice_mask` or of `grounded_mask` on one device may be relied on, other than what follows from the above.
Results may differ from the reference program's by a relative error of at most 0.0003.
Values sent between devices are 32-bit elements; how exact they have to be, the bound alone decides.
A program may use at most 64 MiB of HBM per device.

```python
import math
import jax
import jax.numpy as jnp
from jax import lax

MEMBERS = 8
NX = 1024
NY = 4096


def draw_thickness(key, part):
    rows = jnp.arange(NX, dtype=jnp.float32)[:, None] / float(max(NX - 1, 1))
    rough = jax.random.uniform(key, (NX, NY), jnp.float32, 0.5, 1.5)
    trend = 1.0 + 2.0 * rows
    return trend * rough


def draw_surface(key, part):
    rough = jax.random.truncated_normal(key, -4.0, 4.0, (NX, NY), jnp.float32)
    return rough


def plant(entries, own_key, least, top_value):
    index_at = [jax.random.randint(jax.random.fold_in(own_key, axis), (), 0, length) for axis, length in enumerate(entries.shape)]
    widest = entries.shape.index(max(entries.shape))
    beside = index_at[:widest] + [(index_at[widest] + 1) % entries.shape[widest]] + index_at[widest + 1:]
    return entries.at[tuple(index_at)].set(least).at[tuple(beside)].set(top_value)


def level_of(rng, shape, shards, low, largest):
    loudness = 1.0
    for position, parts in shards:
        steps = jax.random.uniform(jax.random.fold_in(jax.random.fold_in(rng, 6), position), (parts,), jnp.float32, low / len(shards), largest / len(shards))
        loudness = loudness * jnp.repeat(jnp.exp(steps), shape[position] // parts).reshape((-1,) + (1,) * (len(shape) - 1 - position))
    return loudness


def scatter_about(key, dims, spread, bound, shards=(), kind=jnp.bfloat16):
    gain = level_of(key, dims, shards, -0.22, 0.18) if shards else 1.0
    entries = jax.random.normal(key, dims, jnp.float32) * spread * gain
    return jnp.minimum(jnp.maximum(entries, -bound), bound).astype(kind)


def setup_inputs(seed: int = 0) -> dict:
    key_list = jax.random.split(jax.random.key(seed), 7)
    return {
        "velocity_guess": scatter_about(key_list[0], (MEMBERS, 2, NX, NY), 1.0, 6.0, ((2, 32), (3, 16)), jnp.float32),
        "friction": jnp.clip(jnp.exp(math.log(4.0) - 2.0794415 * jax.random.uniform(key_list[1], (MEMBERS, NX, NY), jnp.float32) ** level_of(key_list[1], (MEMBERS, NX, NY), ((1, 32), (2, 16)), -0.2, 0.2)), 0.5, 4.0).astype(jnp.bfloat16),
        "thickness": draw_thickness(jax.random.fold_in(key_list[6], 71), 0),
        "surface": draw_surface(jax.random.fold_in(key_list[6], 71), 0),
        "ice_mask": plant((jax.random.randint(key_list[4], (NX, NY), 0, 8) < 7).astype(jnp.int32), jax.random.fold_in(key_list[4], 1), 0, 1),
        "grounded_mask": plant((jax.random.randint(key_list[5], (NX, NY), 0, 2) < 1).astype(jnp.int32), jax.random.fold_in(key_list[5], 1), 0, 1),
    }


strain_floor = 0.1
water_drag = 0.25
flow_power = 1.0 / 3.0


def diff_rows(field):
    padded = jnp.pad(field, ((1, 1), (0, 0)))
    return 0.5 * (padded[2:] - padded[:-2])


def diff_cols(field):
    padded = jnp.pad(field, ((0, 0), (1, 1)))
    return 0.5 * (padded[:, 2:] - padded[:, :-2])


def strains(field_u, field_v):
    return diff_rows(field_u), diff_cols(field_v), diff_cols(field_u) + diff_rows(field_v)


def reference(velocity_guess, friction, thickness, surface, ice_mask, grounded_mask):
    icef = ice_mask.astype(jnp.float32)
    groundf = grounded_mask.astype(jnp.float32)
    force_u = icef * (-(thickness * diff_rows(surface)))
    force_v = icef * (-(thickness * diff_cols(surface)))

    def member(item):
        guess, fric = item
        drag = icef * (groundf * fric.astype(jnp.float32) + water_drag)
        start_u = icef * guess[0]
        start_v = icef * guess[1]
        sa, sb, sc = strains(start_u, start_v)
        nu = icef * 0.5 * thickness * jnp.power(sa * sa + sb * sb + sa * sb + 0.25 * (sc * sc) + strain_floor, -flow_power)
        padnu = jnp.pad(nu, 1)
        near_rows = padnu[2:, 1:-1] + padnu[:-2, 1:-1]
        near_cols = padnu[1:-1, 2:] + padnu[1:-1, :-2]
        prec_u = icef * (near_rows + 0.25 * near_cols + drag) + (1.0 - icef)
        prec_v = icef * (near_cols + 0.25 * near_rows + drag) + (1.0 - icef)

        def operate(part_u, part_v):
            ka, kb, kc = strains(part_u, part_v)
            sxx = nu * (4.0 * ka + 2.0 * kb)
            syy = nu * (2.0 * ka + 4.0 * kb)
            sxy = nu * kc
            return (icef * (drag * part_u - diff_rows(sxx) - diff_cols(sxy)),
                    icef * (drag * part_v - diff_cols(syy) - diff_rows(sxy)))

        vel_u, vel_v = start_u, start_v
        image_u, image_v = operate(start_u, start_v)
        res_u = force_u - image_u
        res_v = force_v - image_v
        pre_u = res_u / prec_u
        pre_v = res_v / prec_v
        dir_u, dir_v = pre_u, pre_v
        norm_now = jnp.sum(res_u * pre_u) + jnp.sum(res_v * pre_v)
        for step in range(2):
            image_u, image_v = operate(dir_u, dir_v)
            alpha = norm_now / (jnp.sum(dir_u * image_u) + jnp.sum(dir_v * image_v))
            vel_u = vel_u + alpha * dir_u
            vel_v = vel_v + alpha * dir_v
            res_u = res_u - alpha * image_u
            res_v = res_v - alpha * image_v
            if step == 0:
                pre_u = res_u / prec_u
                pre_v = res_v / prec_v
                norm_next = jnp.sum(res_u * pre_u) + jnp.sum(res_v * pre_v)
                dir_u = pre_u + (norm_next / norm_now) * dir_u
                dir_v = pre_v + (norm_next / norm_now) * dir_v
                norm_now = norm_next
        return jnp.stack([vel_u, vel_v])

    return lax.map(member, (velocity_guess, friction))
```

```python
import jax
import jax.numpy as jnp
from jax import lax
from jax.experimental import pallas as pl
from jax.experimental.pallas import tpu as pltpu
from jax.sharding import PartitionSpec as P

MESH = pl.DeviceIdType.MESH
F32 = jnp.float32

strain_floor = 0.1
water_drag = 0.25
flow_power = 1.0 / 3.0

GUESS_W, DRAG_W, FLAT_W = 5, 3, 4
MEMBER_LANES = 2 * (GUESS_W + GUESS_W + DRAG_W)
U_AT, V_AT, DRAG_AT = GUESS_W, 3 * GUESS_W, 4 * GUESS_W + DRAG_W
PER_TILE = 4
FLAT_AT = PER_TILE * MEMBER_LANES + FLAT_W
EDGE = 8
LANES = 128


def neighbours():
    rows, cols = lax.axis_size("gx"), lax.axis_size("gy")
    me_x, me_y = lax.axis_index("gx"), lax.axis_index("gy")
    up, down = lax.rem(me_x + rows - 1, rows), lax.rem(me_x + 1, rows)
    left, right = lax.rem(me_y + cols - 1, cols), lax.rem(me_y + 1, cols)
    return me_x, me_y, up, down, left, right


def shift(cells, by, axis):
    return pltpu.roll(cells, by % cells.shape[axis], axis)


def diff(cells, axis):
    return shift(cells, -1, axis) - shift(cells, 1, axis)


def near(cells, axis):
    return shift(cells, -1, axis) + shift(cells, 1, axis)


def row_places(members):
    guess = [GUESS_W * i for i in range(2 * members)]
    drag = [GUESS_W * 2 * members + DRAG_W * i for i in range(members)]
    flat = GUESS_W * 2 * members + DRAG_W * members
    return guess, drag, (flat, flat + FLAT_W), flat + 2 * FLAT_W


def halo_kernel(guess_ref, fric_ref, thick_ref, surf_ref, ice_ref, ground_ref,
                from_up, from_down, from_left, from_right,
                go_up, go_down, go_left, go_right, in_up, in_down, in_left, in_right, send_sem, recv_sem):
    me_x, me_y, up, down, left, right = neighbours()
    around = [(up, me_y), (down, me_y), (me_x, left), (me_x, right),
              (up, left), (up, right), (down, left), (down, right)]
    barrier = pltpu.get_barrier_semaphore()
    for place in around:
        pl.semaphore_signal(barrier, inc=1, device_id=place, device_id_type=MESH)

    members, _, rows, cols = guess_ref.shape
    ice = ice_ref[...].astype(F32)
    ground = ground_ref[...].astype(F32)
    thick = ice * thick_ref[...]
    surf = surf_ref[...]
    go_left[...] = jnp.zeros_like(go_left)
    go_right[...] = jnp.zeros_like(go_right)
    guess_at, drag_at, flat_at, _ = row_places(members)
    lane = lax.broadcasted_iota(jnp.int32, (rows, LANES), 1)

    def pack_cols(tile, cells, at, width):
        head = shift(cells[:, :LANES], at, 1)
        tail = shift(cells[:, cols - LANES:], at, 1)
        go_left[tile] = jnp.where((lane >= at) & (lane < at + width), head, go_left[tile])
        go_right[tile] = jnp.where((lane >= at - width) & (lane < at), tail, go_right[tile])

    def pack_rows(cells, at, width):
        go_up[at:at + width, :] = cells[:width, :]
        go_down[at:at + width, :] = cells[rows - width:, :]

    for m in range(members):
        tile, base = m // PER_TILE, (m % PER_TILE) * MEMBER_LANES
        u, v = ice * guess_ref[m, 0], ice * guess_ref[m, 1]
        drag = ice * (ground * fric_ref[m].astype(F32) + water_drag)
        pack_rows(u, guess_at[2 * m], GUESS_W)
        pack_rows(v, guess_at[2 * m + 1], GUESS_W)
        pack_rows(drag, drag_at[m], DRAG_W)
        pack_cols(tile, u, base + U_AT, GUESS_W)
        pack_cols(tile, v, base + V_AT, GUESS_W)
        pack_cols(tile, drag, base + DRAG_AT, DRAG_W)
    pack_rows(thick, flat_at[0], FLAT_W)
    pack_rows(surf, flat_at[1], FLAT_W)
    pack_cols(0, thick, FLAT_AT, FLAT_W)
    pack_cols(1, surf, FLAT_AT, FLAT_W)

    pl.semaphore_wait(barrier, len(around))
    top, mid, low = pl.ds(0, EDGE), pl.ds(EDGE, rows), pl.ds(EDGE + rows, EDGE)
    first, final = pl.ds(0, EDGE), pl.ds(rows - EDGE, EDGE)
    moves = [
        (go_up, in_down),
        (go_down, in_up),
        (go_left, in_right.at[:, mid]),
        (go_right, in_left.at[:, mid]),
        (go_left.at[:, first], in_right.at[:, low]),
        (go_right.at[:, first], in_left.at[:, low]),
        (go_left.at[:, final], in_right.at[:, top]),
        (go_right.at[:, final], in_left.at[:, top]),
    ]
    copies = [
        pltpu.make_async_remote_copy(
            src_ref=source, dst_ref=target, send_sem=send_sem.at[i], recv_sem=recv_sem.at[i],
            device_id=around[i], device_id_type=MESH)
        for i, (source, target) in enumerate(moves)
    ]
    for copy in copies:
        copy.start()
    for copy in copies:
        copy.wait()
    from_up[...] = in_up[...]
    from_down[...] = in_down[...]
    from_left[...] = in_left[...]
    from_right[...] = in_right[...]


def solve_kernel(guess_ref, fric_ref, thick_ref, surf_ref, ice_ref, ground_ref,
                 from_up, from_down, from_left, from_right,
                 z_ref, y_ref, sums_ref,
                 guess_ext, drag_ext, thick_ext, surf_ext, strip):
    members, _, rows, cols = guess_ref.shape
    me_x, me_y = lax.axis_index("gx"), lax.axis_index("gy")
    is_top, is_low = me_x == 0, me_x == lax.axis_size("gx") - 1
    is_left, is_right = me_y == 0, me_y == lax.axis_size("gy") - 1
    guess_at, drag_at, flat_at, _ = row_places(members)
    high = rows + 2 * EDGE

    row = lax.broadcasted_iota(jnp.int32, (high, LANES), 0)
    outside = (is_top & (row < EDGE)) | (is_low & (row >= EDGE + rows))
    for tile in range(2):
        left = jnp.where(is_left, 0.0, from_left[tile])
        right = jnp.where(is_right, 0.0, from_right[tile])
        strip[tile] = jnp.where(outside, 0.0, left + right)

    ice = ice_ref[...].astype(F32)
    ground = ground_ref[...].astype(F32)

    def fill(ext, cells, at, width, tile, lane_at):
        ext[EDGE:EDGE + rows, :cols] = cells
        ext[EDGE - width:EDGE, :cols] = jnp.where(is_top, 0.0, from_up[at:at + width, :])
        ext[EDGE + rows:EDGE + rows + width, :cols] = jnp.where(is_low, 0.0, from_down[at:at + width, :])
        ext[:, cols:] = shift(strip[tile], -lane_at, 1)

    for m in range(members):
        tile, base = m // PER_TILE, (m % PER_TILE) * MEMBER_LANES
        fill(guess_ext.at[m, 0], ice * guess_ref[m, 0], guess_at[2 * m], GUESS_W, tile, base + U_AT)
        fill(guess_ext.at[m, 1], ice * guess_ref[m, 1], guess_at[2 * m + 1], GUESS_W, tile, base + V_AT)
        drag = ice * (ground * fric_ref[m].astype(F32) + water_drag)
        fill(drag_ext.at[m], drag, drag_at[m], DRAG_W, tile, base + DRAG_AT)
    fill(thick_ext, ice * thick_ref[...], flat_at[0], FLAT_W, 0, FLAT_AT)
    fill(surf_ext, surf_ref[...], flat_at[1], FLAT_W, 1, FLAT_AT)

    def member(m, carry):
        thick = thick_ext[...]
        surf = surf_ext[...]
        on_ice = thick > 0.0
        half = 0.5 * thick
        u, v, drag = guess_ext[m, 0], guess_ext[m, 1], drag_ext[m]

        def strains(pu, pv):
            return diff(pu, 0), diff(pv, 1), diff(pu, 1) + diff(pv, 0)

        def form(a, b, c):
            return a * a + b * b + a * b + 0.25 * (c * c)

        def operate(nu_half, pu, pv, a, b, c):
            sxx = nu_half * (2.0 * a + b)
            syy = nu_half * (a + 2.0 * b)
            sxy = nu_half * (0.5 * c)
            return (drag * pu - diff(sxx, 0) - diff(sxy, 1),
                    drag * pv - diff(syy, 1) - diff(sxy, 0))

        a, b, c = strains(u, v)
        nu = half * jnp.exp(-flow_power * jnp.log(0.25 * form(a, b, c) + strain_floor))
        nu_half = 0.5 * nu
        near_rows, near_cols = near(nu, 0), near(nu, 1)
        inv_u = jnp.where(on_ice, 1.0 / (near_rows + 0.25 * near_cols + drag), 0.0)
        inv_v = jnp.where(on_ice, 1.0 / (near_cols + 0.25 * near_rows + drag), 0.0)
        image_u, image_v = operate(nu_half, u, v, a, b, c)
        res_u = -(half * diff(surf, 0)) - image_u
        res_v = -(half * diff(surf, 1)) - image_v
        z_u, z_v = res_u * inv_u, res_v * inv_v
        a, b, c = strains(z_u, z_v)
        image_u, image_v = operate(nu_half, z_u, z_v, a, b, c)
        gap_u, gap_v = image_u - res_u, image_v - res_v
        y_u, y_v = gap_u * inv_u, gap_v * inv_v
        a, b, c = strains(y_u, y_v)
        energy = nu * form(a, b, c) + drag * (y_u * y_u + y_v * y_v)

        def own(cells):
            return cells[EDGE:EDGE + rows, :cols]

        z_ref[m, 0] = own(z_u)
        z_ref[m, 1] = own(z_v)
        y_ref[m, 0] = own(y_u)
        y_ref[m, 1] = own(y_v)
        lane = lax.broadcasted_iota(jnp.int32, (1, LANES), 1)
        line = jnp.zeros((1, LANES), F32)
        for i, cells in enumerate((res_u * z_u + res_v * z_v, res_u * y_u + res_v * y_v,
                                   gap_u * y_u + gap_v * y_v, energy)):
            total = jnp.sum(own(cells), axis=(0, 1), keepdims=True)
            line = jnp.where(lane == i, total, line)
        sums_ref[pl.ds(m, 1), :] = line
        return carry

    lax.fori_loop(0, members, member, 0)


def groups(rows, cols):
    fine = 4 if rows % 4 == 0 else 1
    pair = 2 if cols % 2 == 0 else 1
    me_x, me_y = lax.axis_index("gx"), lax.axis_index("gy")
    deep, wide = me_x // fine, lax.rem(me_x, fine)
    tall, core = me_y // pair, lax.rem(me_y, pair)

    def chips(step):
        rank = lax.rem(wide * pair + core + step, fine * pair)
        return deep * fine + rank // pair, tall * pair + lax.rem(rank, pair)

    def along_y(step):
        return me_x, lax.rem(tall + step, cols // pair) * pair + core

    def along_z(step):
        return lax.rem(deep + step, rows // fine) * fine + wide, me_y

    return [(fine * pair, wide * pair + core, chips), (cols // pair, tall, along_y), (rows // fine, deep, along_z)]


def sum_kernel(sums_ref, out_ref, held, send_sem, recv_sem):
    phases = groups(lax.axis_size("gx"), lax.axis_size("gy"))
    barrier = pltpu.get_barrier_semaphore()
    count = 0
    for size, _, place in phases:
        for step in range(1, size):
            pl.semaphore_signal(barrier, inc=1, device_id=place(step), device_id_type=MESH)
            count += 1
    pl.semaphore_wait(barrier, count)
    total = sums_ref[...]
    for phase, (size, me, place) in enumerate(phases):
        if size == 1:
            continue
        slots = held.at[phase]
        slots[me] = total
        copies = [
            pltpu.make_async_remote_copy(
                src_ref=slots.at[me], dst_ref=slots.at[me], send_sem=send_sem.at[phase, step],
                recv_sem=recv_sem.at[phase, step], device_id=place(step), device_id_type=MESH)
            for step in range(1, size)
        ]
        for copy in copies:
            copy.start()
        for copy in copies:
            copy.wait_recv()
        total = slots[0]
        for i in range(1, size):
            total = total + slots[i]
        for copy in copies:
            copy.wait_send()
    rz, cross, square, energy = (total[:, i:i + 1] for i in range(4))
    scale = rz + cross
    alpha = rz / scale
    mixed = cross + square
    eta = mixed / scale
    top = square - cross * cross / rz
    low = energy - mixed * eta
    step_two = jnp.where(low > 0.0, jnp.maximum(top, 0.0) / low, 0.0)
    lane = lax.broadcasted_iota(jnp.int32, total.shape, 1)
    out_ref[...] = jnp.where(lane == 0, alpha * (1.0 + step_two * eta), -(alpha * step_two))


def per_device(velocity_guess, friction, thickness, surface, ice_mask, grounded_mask):
    members, _, rows, cols = velocity_guess.shape
    fields = (velocity_guess, friction, thickness, surface, ice_mask, grounded_mask)
    packed = row_places(members)[3]
    high = rows + 2 * EDGE
    vmem = pl.BlockSpec(memory_space=pltpu.VMEM)
    line = jax.ShapeDtypeStruct((packed, cols), F32)
    side = jax.ShapeDtypeStruct((2, high, LANES), F32)
    edges = pl.pallas_call(
        halo_kernel,
        out_shape=(line, line, side, side),
        in_specs=[vmem] * 6,
        out_specs=(vmem,) * 4,
        scratch_shapes=[
            pltpu.VMEM((packed, cols), F32), pltpu.VMEM((packed, cols), F32),
            pltpu.VMEM((2, rows, LANES), F32), pltpu.VMEM((2, rows, LANES), F32),
            pltpu.VMEM((packed, cols), F32), pltpu.VMEM((packed, cols), F32),
            pltpu.VMEM((2, high, LANES), F32), pltpu.VMEM((2, high, LANES), F32),
            pltpu.SemaphoreType.DMA((8,)), pltpu.SemaphoreType.DMA((8,)),
        ],
        compiler_params=pltpu.CompilerParams(collective_id=0, has_side_effects=True),
        name="halo",
    )(*fields)
    wide = cols + LANES
    block = jax.ShapeDtypeStruct((members, 2, rows, cols), F32)
    z, y, sums = pl.pallas_call(
        solve_kernel,
        out_shape=(block, block, jax.ShapeDtypeStruct((members, LANES), F32)),
        in_specs=[vmem] * 10,
        out_specs=(vmem,) * 3,
        scratch_shapes=[
            pltpu.VMEM((members, 2, high, wide), F32), pltpu.VMEM((members, high, wide), F32),
            pltpu.VMEM((high, wide), F32), pltpu.VMEM((high, wide), F32),
            pltpu.VMEM((2, high, LANES), F32),
        ],
        compiler_params=pltpu.CompilerParams(vmem_limit_bytes=48 << 20),
        name="solve",
    )(*fields, *edges)
    coefs = pl.pallas_call(
        sum_kernel,
        out_shape=jax.ShapeDtypeStruct((members, LANES), F32),
        in_specs=[vmem],
        out_specs=vmem,
        scratch_shapes=[
            pltpu.VMEM((3, 8, members, LANES), F32),
            pltpu.SemaphoreType.DMA((3, 8)), pltpu.SemaphoreType.DMA((3, 8)),
        ],
        compiler_params=pltpu.CompilerParams(collective_id=1, has_side_effects=True),
        name="sum_all",
    )(sums)
    first, second = coefs[:, 0, None, None, None], coefs[:, 1, None, None, None]
    return ice_mask.astype(F32) * velocity_guess + (first * z + second * y)


def solution(mesh):
    placed = (
        P(None, None, "gx", "gy"),
        P(None, "gx", "gy"),
        P("gx", "gy"),
        P("gx", "gy"),
        P("gx", "gy"),
        P("gx", "gy"),
    )
    return jax.shard_map(
        per_device, mesh=mesh, in_specs=placed, out_specs=P(None, None, "gx", "gy"), check_vma=False
    )
```

```python
import itertools

import jax
import jax.numpy as jnp
from jax import lax
from jax.experimental import pallas as pl
from jax.experimental.pallas import tpu as pltpu
from jax.sharding import PartitionSpec as P

MESH = pl.DeviceIdType.MESH
F32 = jnp.float32

strain_floor = 0.1
water_drag = 0.25
flow_power = 1.0 / 3.0

GUESS_W, DRAG_W, FLAT_W = 5, 3, 4
MEMBER_LANES = 2 * (GUESS_W + GUESS_W + DRAG_W)
U_AT, V_AT, DRAG_AT = GUESS_W, 3 * GUESS_W, 4 * GUESS_W + DRAG_W
PER_TILE = 4
FLAT_AT = PER_TILE * MEMBER_LANES + FLAT_W
EDGE = 8
LANES = 128
QUARTER = LANES // 4


def neighbours():
    rows, cols = lax.axis_size("gx"), lax.axis_size("gy")
    me_x, me_y = lax.axis_index("gx"), lax.axis_index("gy")
    up, down = lax.rem(me_x + rows - 1, rows), lax.rem(me_x + 1, rows)
    left, right = lax.rem(me_y + cols - 1, cols), lax.rem(me_y + 1, cols)
    return me_x, me_y, up, down, left, right


def shift(cells, by, axis):
    return pltpu.roll(cells, by % cells.shape[axis], axis)


def diff(cells, axis):
    return shift(cells, -1, axis) - shift(cells, 1, axis)


def near(cells, axis):
    return shift(cells, -1, axis) + shift(cells, 1, axis)


def row_places(members):
    guess = [GUESS_W * i for i in range(2 * members)]
    drag = [GUESS_W * 2 * members + DRAG_W * i for i in range(members)]
    flat = GUESS_W * 2 * members + DRAG_W * members
    return guess, drag, (flat, flat + FLAT_W), flat + 2 * FLAT_W


def spread(axes):
    sizes = [size for size, _, _ in axes]
    place = 0
    for size, mine, _ in axes:
        place = place * size + mine
    steps = [step for step in itertools.product(*map(range, sizes)) if any(step)]

    def reach(step):
        return sum(min(by, size - by) * far for by, (size, _, far) in zip(step, axes))

    steps.sort(key=lambda step: -reach(step))
    return place, [[lax.rem(mine + by, size) for by, (size, mine, _) in zip(step, axes)] for step in steps]


def groups():
    rows, cols = lax.axis_size("gx"), lax.axis_size("gy")
    fine = 4 if rows % 4 == 0 else 1
    pair = 2 if cols % 2 == 0 else 1
    me_x, me_y = lax.axis_index("gx"), lax.axis_index("gy")
    place_y, others_y = spread([(cols // pair, me_y // pair, 1.0), (pair, lax.rem(me_y, pair), 0.1)])
    place_x, others_x = spread([(rows // fine, me_x // fine, 1.0), (fine, lax.rem(me_x, fine), 1.0)])
    return [
        (cols, place_y, [(me_x, chip * pair + core) for chip, core in others_y]),
        (rows, place_x, [(deep * fine + wide, me_y) for deep, wide in others_x]),
    ]


def kernel(guess_hbm, fric_hbm, thick_hbm, surf_hbm, ice_hbm, ground_hbm, out_ref,
           guess_ref, fric_ref, thick_ref, surf_ref, ice_ref, ground_ref,
           go_up, go_down, go_left, go_right, in_up, in_down, in_left, in_right,
           guess_ext, drag_ext, thick_ext, surf_ext, strip, z_ref, y_ref, held,
           load_sem, send_sem, recv_sem, push_sem, pull_sem):
    me_x, me_y, up, down, left, right = neighbours()
    around = [(up, me_y), (down, me_y), (me_x, left), (me_x, right),
              (up, left), (up, right), (down, left), (down, right)]
    phases = groups()
    sources = (ice_hbm, ground_hbm, thick_hbm, surf_hbm, guess_hbm, fric_hbm)
    targets = (ice_ref, ground_ref, thick_ref, surf_ref, guess_ref, fric_ref)
    loads = [pltpu.make_async_copy(source, target, load_sem.at[i])
             for i, (source, target) in enumerate(zip(sources, targets))]
    for load in loads:
        load.start()

    barrier = pltpu.get_barrier_semaphore()
    greeted = [place for _, _, others in phases[::-1] for place in others] + around
    for place in greeted:
        pl.semaphore_signal(barrier, inc=1, device_id=place, device_id_type=MESH)

    members, _, rows, cols = guess_ref.shape
    high = rows + 2 * EDGE
    is_top, is_low = me_x == 0, me_x == lax.axis_size("gx") - 1
    is_left, is_right = me_y == 0, me_y == lax.axis_size("gy") - 1
    guess_at, drag_at, flat_at, _ = row_places(members)

    go_left[...] = jnp.zeros_like(go_left)
    go_right[...] = jnp.zeros_like(go_right)
    for load in loads:
        load.wait()
    ice = ice_ref[...].astype(F32)
    ground = ground_ref[...].astype(F32)
    lane = lax.broadcasted_iota(jnp.int32, (rows, LANES), 1)

    def pack(ext, cells, row_at, width, tile, lane_at):
        ext[EDGE:EDGE + rows, :cols] = cells
        go_up[row_at:row_at + width, :] = cells[:width, :]
        go_down[row_at:row_at + width, :] = cells[rows - width:, :]
        head = shift(cells[:, :LANES], lane_at, 1)
        tail = shift(cells[:, cols - LANES:], lane_at, 1)
        go_left[tile] = jnp.where((lane >= lane_at) & (lane < lane_at + width), head, go_left[tile])
        go_right[tile] = jnp.where((lane >= lane_at - width) & (lane < lane_at), tail, go_right[tile])

    def every_field(act):
        for m in range(members):
            tile, base = m // PER_TILE, (m % PER_TILE) * MEMBER_LANES
            act(guess_ext.at[m, 0], lambda: ice * guess_ref[m, 0], guess_at[2 * m], GUESS_W, tile, base + U_AT)
            act(guess_ext.at[m, 1], lambda: ice * guess_ref[m, 1], guess_at[2 * m + 1], GUESS_W, tile, base + V_AT)
            act(drag_ext.at[m], lambda: ice * (ground * fric_ref[m].astype(F32) + water_drag),
                drag_at[m], DRAG_W, tile, base + DRAG_AT)
        act(thick_ext, lambda: ice * thick_ref[...], flat_at[0], FLAT_W, 0, FLAT_AT)
        act(surf_ext, lambda: surf_ref[...], flat_at[1], FLAT_W, 1, FLAT_AT)

    every_field(lambda ext, cells, *where: pack(ext, cells(), *where))

    pl.semaphore_wait(barrier, len(greeted))
    above, mid, below = pl.ds(0, EDGE), pl.ds(EDGE, rows), pl.ds(EDGE + rows, EDGE)
    first, final = pl.ds(0, EDGE), pl.ds(rows - EDGE, EDGE)
    moves = [
        (go_up, in_down),
        (go_down, in_up),
        (go_left, in_right.at[:, mid]),
        (go_right, in_left.at[:, mid]),
        (go_left.at[:, first], in_right.at[:, below]),
        (go_right.at[:, first], in_left.at[:, below]),
        (go_left.at[:, final], in_right.at[:, above]),
        (go_right.at[:, final], in_left.at[:, above]),
    ]
    copies = [
        pltpu.make_async_remote_copy(
            src_ref=source, dst_ref=target, send_sem=send_sem.at[i], recv_sem=recv_sem.at[i],
            device_id=around[i], device_id_type=MESH)
        for i, (source, target) in enumerate(moves)
    ]
    for copy in copies:
        copy.start()
    for copy in copies:
        copy.wait_recv()

    row = lax.broadcasted_iota(jnp.int32, (high, LANES), 0)
    outside = (is_top & (row < EDGE)) | (is_low & (row >= EDGE + rows))
    for tile in range(2):
        west = jnp.where(is_left, 0.0, in_left[tile])
        east = jnp.where(is_right, 0.0, in_right[tile])
        strip[tile] = jnp.where(outside, 0.0, west + east)

    def fill(ext, cells, row_at, width, tile, lane_at):
        ext[EDGE - width:EDGE, :cols] = jnp.where(is_top, 0.0, in_up[row_at:row_at + width, :])
        ext[EDGE + rows:EDGE + rows + width, :cols] = jnp.where(is_low, 0.0, in_down[row_at:row_at + width, :])
        ext[:, cols:] = shift(strip[tile], -lane_at, 1)

    every_field(fill)

    def member(m, line):
        thick = thick_ext[...]
        surf = surf_ext[...]
        on_ice = thick > 0.0
        half = 0.5 * thick
        u, v, drag = guess_ext[m, 0], guess_ext[m, 1], drag_ext[m]

        def strains(pu, pv):
            return diff(pu, 0), diff(pv, 1), diff(pu, 1) + diff(pv, 0)

        def form(a, b, c):
            return a * a + b * b + a * b + 0.25 * (c * c)

        def operate(nu_half, pu, pv, a, b, c):
            sxx = nu_half * (2.0 * a + b)
            syy = nu_half * (a + 2.0 * b)
            sxy = nu_half * (0.5 * c)
            return (drag * pu - diff(sxx, 0) - diff(sxy, 1),
                    drag * pv - diff(syy, 1) - diff(sxy, 0))

        a, b, c = strains(u, v)
        nu = half * jnp.exp(-flow_power * jnp.log(0.25 * form(a, b, c) + strain_floor))
        nu_half = 0.5 * nu
        near_rows, near_cols = near(nu, 0), near(nu, 1)
        inv_u = jnp.where(on_ice, 1.0 / (near_rows + 0.25 * near_cols + drag), 0.0)
        inv_v = jnp.where(on_ice, 1.0 / (near_cols + 0.25 * near_rows + drag), 0.0)
        image_u, image_v = operate(nu_half, u, v, a, b, c)
        res_u = -(half * diff(surf, 0)) - image_u
        res_v = -(half * diff(surf, 1)) - image_v
        z_u, z_v = res_u * inv_u, res_v * inv_v
        a, b, c = strains(z_u, z_v)
        image_u, image_v = operate(nu_half, z_u, z_v, a, b, c)
        gap_u, gap_v = image_u - res_u, image_v - res_v
        y_u, y_v = gap_u * inv_u, gap_v * inv_v
        a, b, c = strains(y_u, y_v)
        energy = nu * form(a, b, c) + drag * (y_u * y_u + y_v * y_v)

        def own(cells):
            return cells[EDGE:EDGE + rows, :cols]

        z_ref[m, 0] = own(z_u)
        z_ref[m, 1] = own(z_v)
        y_ref[m, 0] = own(y_u)
        y_ref[m, 1] = own(y_v)
        slot = lax.broadcasted_iota(jnp.int32, (1, LANES), 1)
        for i, cells in enumerate((res_u * z_u + res_v * z_v, res_u * y_u + res_v * y_v,
                                   gap_u * y_u + gap_v * y_v, energy)):
            total = jnp.sum(own(cells), axis=(0, 1), keepdims=True)
            line = jnp.where(slot == i * QUARTER + m, total, line)
        return line

    total = lax.fori_loop(0, members, member, jnp.zeros((1, LANES), F32))

    pushes = []
    for phase, (size, me, others) in enumerate(phases):
        slots = held.at[phase]
        slots[me] = total
        batch = [
            pltpu.make_async_remote_copy(
                src_ref=slots.at[me], dst_ref=slots.at[me], send_sem=push_sem.at[phase, i],
                recv_sem=pull_sem.at[phase], device_id=place, device_id_type=MESH)
            for i, place in enumerate(others)
        ]
        for push in batch:
            push.start()
        everything = slots.at[pl.ds(0, size - 1)]
        pltpu.make_async_copy(everything, everything, pull_sem.at[phase]).wait()
        total = slots[0]
        for i in range(1, size):
            total = total + slots[i]
        pushes += batch

    rz, cross, square, energy = (shift(total, -i * QUARTER, 1) for i in range(4))
    scale = rz + cross
    alpha = rz / scale
    mixed = cross + square
    eta = mixed / scale
    top = square - cross * cross / rz
    low = energy - mixed * eta
    step_two = jnp.where(low > 0.0, jnp.maximum(top, 0.0) / low, 0.0)
    to_z, to_y = alpha * (1.0 + step_two * eta), -(alpha * step_two)
    for m in range(members):
        by_z, by_y = to_z[:, m:m + 1], to_y[:, m:m + 1]
        for i in range(2):
            out_ref[m, i] = guess_ext[m, i, EDGE:EDGE + rows, :cols] + (by_z * z_ref[m, i] + by_y * y_ref[m, i])
    for copy in copies + pushes:
        copy.wait_send()


def per_device(velocity_guess, friction, thickness, surface, ice_mask, grounded_mask):
    members, _, rows, cols = velocity_guess.shape
    fields = (velocity_guess, friction, thickness, surface, ice_mask, grounded_mask)
    packed = row_places(members)[3]
    high, wide = rows + 2 * EDGE, cols + LANES
    count_x, count_y = lax.axis_size("gx"), lax.axis_size("gy")
    most = max(count_x, count_y)
    line, block, side = (packed, cols), (2, rows, LANES), (2, high, LANES)
    field = (members, 2, rows, cols)
    return pl.pallas_call(
        kernel,
        out_shape=jax.ShapeDtypeStruct(field, F32),
        in_specs=[pl.BlockSpec(memory_space=pltpu.HBM)] * 6,
        out_specs=pl.BlockSpec(memory_space=pltpu.VMEM),
        scratch_shapes=[pltpu.VMEM(array.shape, array.dtype) for array in fields]
        + [pltpu.VMEM(shape, F32) for shape in (
            line, line, block, block, line, line, side, side,
            (members, 2, high, wide), (members, high, wide), (high, wide), (high, wide), side,
            field, field, (2, most, 1, LANES))]
        + [pltpu.SemaphoreType.DMA((6,)), pltpu.SemaphoreType.DMA((8,)), pltpu.SemaphoreType.DMA((8,)),
           pltpu.SemaphoreType.DMA((2, most)), pltpu.SemaphoreType.DMA((2,))],
        compiler_params=pltpu.CompilerParams(
            collective_id=0, has_side_effects=True, vmem_limit_bytes=60 << 20),
        name="ice",
    )(*fields)


def solution(mesh):
    placed = (
        P(None, None, "gx", "gy"),
        P(None, "gx", "gy"),
        P("gx", "gy"),
        P("gx", "gy"),
        P("gx", "gy"),
        P("gx", "gy"),
    )
    return jax.shard_map(
        per_device, mesh=mesh, in_specs=placed, out_specs=P(None, None, "gx", "gy"), check_vma=False
    )
```

```python
import itertools

import jax
import jax.numpy as jnp
from jax import lax
from jax.experimental import pallas as pl
from jax.experimental.pallas import tpu as pltpu
from jax.sharding import PartitionSpec as P

MESH = pl.DeviceIdType.MESH
F32 = jnp.float32

strain_floor = 0.1
water_drag = 0.25
flow_power = 1.0 / 3.0

GUESS_W, DRAG_W, FLAT_W = 5, 3, 4
MEMBER_LANES = 2 * (GUESS_W + GUESS_W + DRAG_W)
U_AT, V_AT, DRAG_AT = GUESS_W, 3 * GUESS_W, 4 * GUESS_W + DRAG_W
PER_TILE = 4
FLAT_AT = PER_TILE * MEMBER_LANES + FLAT_W
EDGE, HALF = 8, 4
LANES, TILES = 128, 2
QUARTER = LANES // 4


def neighbours():
    rows, cols = lax.axis_size("gx"), lax.axis_size("gy")
    me_x, me_y = lax.axis_index("gx"), lax.axis_index("gy")
    up, down = lax.rem(me_x + rows - 1, rows), lax.rem(me_x + 1, rows)
    left, right = lax.rem(me_y + cols - 1, cols), lax.rem(me_y + 1, cols)
    return me_x, me_y, up, down, left, right


def shift(cells, by, axis):
    return pltpu.roll(cells, by % cells.shape[axis], axis)


def beside(tiles, count):
    lane = lax.broadcasted_iota(jnp.int32, tiles[0].shape, 1)
    ahead = [shift(tile, -1, 1) for tile in tiles]
    behind = [shift(tile, 1, 1) for tile in tiles]
    ring = len(tiles)
    after = [jnp.where(lane == LANES - 1, ahead[(t + 1) % ring], ahead[t]) for t in range(count)]
    before = [jnp.where(lane == 0, behind[t - 1], behind[t]) for t in range(count)]
    return after, before


def diff_cols(tiles, count=3):
    return [ahead - behind for ahead, behind in zip(*beside(tiles, count))]


def form(a, b, c):
    return a * (a + b) + b * b + c * (0.25 * c)


def row_places(members):
    guess = [GUESS_W * i for i in range(2 * members)]
    drag = [GUESS_W * 2 * members + DRAG_W * i for i in range(members)]
    flat = GUESS_W * 2 * members + DRAG_W * members
    return guess, drag, (flat, flat + FLAT_W), flat + 2 * FLAT_W


def spread(axes):
    sizes = [size for size, _, _ in axes]
    place = 0
    for size, mine, _ in axes:
        place = place * size + mine
    steps = [step for step in itertools.product(*map(range, sizes)) if any(step)]

    def reach(step):
        return sum(min(by, size - by) * far for by, (size, _, far) in zip(step, axes))

    steps.sort(key=lambda step: -reach(step))
    return place, [[lax.rem(mine + by, size) for by, (size, mine, _) in zip(step, axes)] for step in steps]


def groups():
    rows, cols = lax.axis_size("gx"), lax.axis_size("gy")
    fine = 4 if rows % 4 == 0 else 1
    pair = 2 if cols % 2 == 0 else 1
    me_x, me_y = lax.axis_index("gx"), lax.axis_index("gy")
    place_y, others_y = spread([(cols // pair, me_y // pair, 1.0), (pair, lax.rem(me_y, pair), 0.1)])
    place_x, others_x = spread([(rows // fine, me_x // fine, 1.0), (fine, lax.rem(me_x, fine), 1.0)])
    return [
        (cols, place_y, [(me_x, chip * pair + core) for chip, core in others_y]),
        (rows, place_x, [(deep * fine + wide, me_y) for deep, wide in others_x]),
    ]


def kernel(guess_hbm, fric_hbm, thick_hbm, surf_hbm, ice_hbm, ground_hbm, out_ref,
           guess_ref, fric_ref, thick_ref, surf_ref, ice_ref, ground_ref,
           go_up, go_down, go_left, go_right, in_up, in_down, in_left, in_right,
           guess_ext, drag_ext, thick_ext, surf_ext, strip, z_ref, y_ref,
           push_u, push_v, nu_ref, sxx_ref, sxy_ref, held,
           load_sem, send_sem, recv_sem, push_sem, pull_sem):
    me_x, me_y, up, down, left, right = neighbours()
    around = [(up, me_y), (down, me_y), (me_x, left), (me_x, right),
              (up, left), (up, right), (down, left), (down, right)]
    phases = groups()
    sources = (ice_hbm, ground_hbm, thick_hbm, surf_hbm, guess_hbm, fric_hbm)
    targets = (ice_ref, ground_ref, thick_ref, surf_ref, guess_ref, fric_ref)
    loads = [pltpu.make_async_copy(source, target, load_sem.at[i])
             for i, (source, target) in enumerate(zip(sources, targets))]
    for load in loads:
        load.start()

    barrier = pltpu.get_barrier_semaphore()
    greeted = [place for _, _, others in phases[::-1] for place in others] + around
    for place in greeted:
        pl.semaphore_signal(barrier, inc=1, device_id=place, device_id_type=MESH)

    members, _, rows, cols = guess_ref.shape
    high = rows + 2 * EDGE
    is_top, is_low = me_x == 0, me_x == lax.axis_size("gx") - 1
    is_left, is_right = me_y == 0, me_y == lax.axis_size("gy") - 1
    guess_at, drag_at, flat_at, _ = row_places(members)

    go_left[...] = jnp.zeros_like(go_left)
    go_right[...] = jnp.zeros_like(go_right)
    for load in loads:
        load.wait()
    ice = ice_ref[...].astype(F32)
    ground = ground_ref[...].astype(F32)
    lane = lax.broadcasted_iota(jnp.int32, (rows, LANES), 1)

    def pack(ext, cells, row_at, width, tile, lane_at):
        for t in range(TILES):
            ext[t, EDGE:EDGE + rows, :] = cells[:, t * LANES:(t + 1) * LANES]
        go_up[row_at:row_at + width, :] = cells[:width, :]
        go_down[row_at:row_at + width, :] = cells[rows - width:, :]
        head = shift(cells[:, :LANES], lane_at, 1)
        tail = shift(cells[:, cols - LANES:], lane_at, 1)
        go_left[tile] = jnp.where((lane >= lane_at) & (lane < lane_at + width), head, go_left[tile])
        go_right[tile] = jnp.where((lane >= lane_at - width) & (lane < lane_at), tail, go_right[tile])

    def every_field(act):
        for m in range(members):
            tile, base = m // PER_TILE, (m % PER_TILE) * MEMBER_LANES
            act(guess_ext.at[m, 0], lambda: ice * guess_ref[m, 0], guess_at[2 * m], GUESS_W, tile, base + U_AT)
            act(guess_ext.at[m, 1], lambda: ice * guess_ref[m, 1], guess_at[2 * m + 1], GUESS_W, tile, base + V_AT)
            act(drag_ext.at[m], lambda: ice * (ground * fric_ref[m].astype(F32) + water_drag),
                drag_at[m], DRAG_W, tile, base + DRAG_AT)
        act(thick_ext, lambda: ice * thick_ref[...], flat_at[0], FLAT_W, 0, FLAT_AT)
        act(surf_ext, lambda: surf_ref[...], flat_at[1], FLAT_W, 1, FLAT_AT)

    every_field(lambda ext, cells, *where: pack(ext, cells(), *where))

    pl.semaphore_wait(barrier, len(greeted))
    above, mid, below = pl.ds(0, EDGE), pl.ds(EDGE, rows), pl.ds(EDGE + rows, EDGE)
    first, final = pl.ds(0, EDGE), pl.ds(rows - EDGE, EDGE)
    moves = [
        (go_up, in_down),
        (go_down, in_up),
        (go_left, in_right.at[:, mid]),
        (go_right, in_left.at[:, mid]),
        (go_left.at[:, first], in_right.at[:, below]),
        (go_right.at[:, first], in_left.at[:, below]),
        (go_left.at[:, final], in_right.at[:, above]),
        (go_right.at[:, final], in_left.at[:, above]),
    ]
    copies = [
        pltpu.make_async_remote_copy(
            src_ref=source, dst_ref=target, send_sem=send_sem.at[i], recv_sem=recv_sem.at[i],
            device_id=around[i], device_id_type=MESH)
        for i, (source, target) in enumerate(moves)
    ]
    for copy in copies:
        copy.start()
    for copy in copies:
        copy.wait_recv()

    row = lax.broadcasted_iota(jnp.int32, (high, LANES), 0)
    outside = (is_top & (row < EDGE)) | (is_low & (row >= EDGE + rows))
    for tile in range(2):
        west = jnp.where(is_left, 0.0, in_left[tile])
        east = jnp.where(is_right, 0.0, in_right[tile])
        strip[tile] = jnp.where(outside, 0.0, west + east)

    def fill(ext, cells, row_at, width, tile, lane_at):
        for t in range(TILES):
            part = slice(t * LANES, (t + 1) * LANES)
            ext[t, EDGE - width:EDGE, :] = jnp.where(is_top, 0.0, in_up[row_at:row_at + width, part])
            ext[t, EDGE + rows:EDGE + rows + width, :] = jnp.where(is_low, 0.0, in_down[row_at:row_at + width, part])
        ext[TILES] = shift(strip[tile], -lane_at, 1)

    every_field(fill)

    zero = me_x // lax.axis_size("gx")
    window, start = rows + 2 * HALF, EDGE - HALF + zero

    def part(ref, tile, by=0):
        return ref[tile, pl.ds(start + by, window), :]

    def tiles_of(ref, by=0):
        return [part(ref, t, by) for t in range(TILES + 1)]

    def diff_rows(ref):
        return [part(ref, t, 1) - part(ref, t, -1) for t in range(TILES + 1)]

    def keep(ref, tiles):
        for t, tile in enumerate(tiles):
            ref[t, pl.ds(start, window), :] = tile

    thick = tiles_of(thick_ext)
    keep(push_u, [0.5 * h * d for h, d in zip(thick, diff_rows(surf_ext))])
    keep(push_v, [0.5 * h * d for h, d in zip(thick, diff_cols(tiles_of(surf_ext)))])

    def strains(u_ref, v_ref):
        u, v = tiles_of(u_ref), tiles_of(v_ref)
        c = [p + q for p, q in zip(diff_cols(u), diff_rows(v_ref))]
        return u, v, diff_rows(u_ref), diff_cols(v), c

    def operate(nu, drag, u, v, a, b, c):
        sxx, syy, sxy = [], [], []
        for n, p, q, w in zip(nu, a, b, c):
            half, both = 0.5 * n, p + q
            sxx.append(half * (p + both))
            syy.append(half * (q + both))
            sxy.append((0.5 * half) * w)
        keep(sxx_ref, sxx)
        keep(sxy_ref, sxy)
        image_u = [d * p - x - y for d, p, x, y in zip(drag, u, diff_rows(sxx_ref), diff_cols(sxy))]
        image_v = [d * p - x - y for d, p, x, y in zip(drag, v, diff_cols(syy), diff_rows(sxy_ref))]
        return image_u, image_v

    own_row = lax.broadcasted_iota(jnp.int32, (window, LANES), 0)
    own_row = (own_row >= HALF) & (own_row < HALF + rows)

    def member(m, line):
        thick = tiles_of(thick_ext)
        drag = tiles_of(drag_ext.at[m])
        u, v, a, b, c = strains(guess_ext.at[m, 0], guess_ext.at[m, 1])
        nu = [(0.5 * h) * jnp.exp(-flow_power * jnp.log(0.25 * form(p, q, w) + strain_floor))
              for h, p, q, w in zip(thick, a, b, c)]
        keep(nu_ref, nu)
        near_rows = [part(nu_ref, t, 1) + part(nu_ref, t, -1) for t in range(TILES + 1)]
        near_cols = [ahead + behind for ahead, behind in zip(*beside(nu, TILES + 1))]
        inv_u = [jnp.where(h > 0.0, 1.0 / (x + 0.25 * y + d), 0.0)
                 for h, x, y, d in zip(thick, near_rows, near_cols, drag)]
        inv_v = [jnp.where(h > 0.0, 1.0 / (y + 0.25 * x + d), 0.0)
                 for h, x, y, d in zip(thick, near_rows, near_cols, drag)]
        image_u, image_v = operate(nu, drag, u, v, a, b, c)
        res_u = [-f - q for f, q in zip(tiles_of(push_u), image_u)]
        res_v = [-f - q for f, q in zip(tiles_of(push_v), image_v)]
        keep(z_ref.at[m, 0], [r * i for r, i in zip(res_u, inv_u)])
        keep(z_ref.at[m, 1], [r * i for r, i in zip(res_v, inv_v)])
        z_u, z_v, a, b, c = strains(z_ref.at[m, 0], z_ref.at[m, 1])
        image_u, image_v = operate(nu, drag, z_u, z_v, a, b, c)
        gap_u = [q - r for q, r in zip(image_u, res_u)]
        gap_v = [q - r for q, r in zip(image_v, res_v)]
        y_u = [g * i for g, i in zip(gap_u, inv_u)]
        y_v = [g * i for g, i in zip(gap_v, inv_v)]
        keep(y_ref.at[m, 0], y_u)
        keep(y_ref.at[m, 1], y_v)

        def own(ref, tile, by=0):
            return ref[tile, pl.ds(EDGE + zero + by, rows), :]

        across_u = diff_cols([own(y_ref.at[m, 0], t) for t in range(TILES + 1)], TILES)
        across_v = diff_cols([own(y_ref.at[m, 1], t) for t in range(TILES + 1)], TILES)
        energy = []
        for t in range(TILES):
            pu, pv = own(y_ref.at[m, 0], t), own(y_ref.at[m, 1], t)
            a = own(y_ref.at[m, 0], t, 1) - own(y_ref.at[m, 0], t, -1)
            c = across_u[t] + own(y_ref.at[m, 1], t, 1) - own(y_ref.at[m, 1], t, -1)
            energy.append(own(nu_ref, t) * form(a, across_v[t], c) + own(drag_ext.at[m], t) * (pu * pu + pv * pv))

        def dot(fu, fv, gu, gv):
            return [jnp.where(own_row, fu[t] * gu[t] + fv[t] * gv[t], 0.0) for t in range(TILES)]

        slot = lax.broadcasted_iota(jnp.int32, (1, LANES), 1)
        for i, cells in enumerate((dot(res_u, res_v, z_u, z_v), dot(res_u, res_v, y_u, y_v),
                                   dot(gap_u, gap_v, y_u, y_v), energy)):
            total = jnp.sum(sum(cells[1:], cells[0]), axis=(0, 1), keepdims=True)
            line = jnp.where(slot == i * QUARTER + m, total, line)
        return line

    total = lax.fori_loop(0, members, member, jnp.zeros((1, LANES), F32), unroll=4)

    pushes = []
    for phase, (size, me, others) in enumerate(phases):
        slots = held.at[phase]
        slots[me] = total
        batch = [
            pltpu.make_async_remote_copy(
                src_ref=slots.at[me], dst_ref=slots.at[me], send_sem=push_sem.at[phase, i],
                recv_sem=pull_sem.at[phase], device_id=place, device_id_type=MESH)
            for i, place in enumerate(others)
        ]
        for push in batch:
            push.start()
        everything = slots.at[pl.ds(0, size - 1)]
        pltpu.make_async_copy(everything, everything, pull_sem.at[phase]).wait()
        total = slots[0]
        for i in range(1, size):
            total = total + slots[i]
        pushes += batch

    rz, cross, square, energy = (shift(total, -i * QUARTER, 1) for i in range(4))
    scale = rz + cross
    alpha = rz / scale
    mixed = cross + square
    eta = mixed / scale
    top = square - cross * cross / rz
    low = energy - mixed * eta
    step_two = jnp.where(low > 0.0, jnp.maximum(top, 0.0) / low, 0.0)
    to_z, to_y = alpha * (1.0 + step_two * eta), -(alpha * step_two)
    for m in range(members):
        by_z, by_y = to_z[:, m:m + 1], to_y[:, m:m + 1]
        for i in range(2):
            for t in range(TILES):
                own = pl.ds(EDGE, rows)
                out_ref[m, i, :, t * LANES:(t + 1) * LANES] = guess_ext[m, i, t, own, :] + (
                    by_z * z_ref[m, i, t, own, :] + by_y * y_ref[m, i, t, own, :])
    for copy in copies + pushes:
        copy.wait_send()


def per_device(velocity_guess, friction, thickness, surface, ice_mask, grounded_mask):
    members, _, rows, cols = velocity_guess.shape
    fields = (velocity_guess, friction, thickness, surface, ice_mask, grounded_mask)
    packed = row_places(members)[3]
    high = rows + 2 * EDGE
    flat = (TILES + 1, high, LANES)
    count_x, count_y = lax.axis_size("gx"), lax.axis_size("gy")
    most = max(count_x, count_y)
    line, block, side = (packed, cols), (2, rows, LANES), (2, high, LANES)
    field = (members, 2, rows, cols)
    return pl.pallas_call(
        kernel,
        out_shape=jax.ShapeDtypeStruct(field, F32),
        in_specs=[pl.BlockSpec(memory_space=pltpu.HBM)] * 6,
        out_specs=pl.BlockSpec(memory_space=pltpu.VMEM),
        scratch_shapes=[pltpu.VMEM(array.shape, array.dtype) for array in fields]
        + [pltpu.VMEM(shape, F32) for shape in (
            line, line, block, block, line, line, side, side,
            (members, 2) + flat, (members,) + flat, flat, flat, side,
            (members, 2) + flat, (members, 2) + flat, flat, flat, flat, flat, flat, (2, most, 1, LANES))]
        + [pltpu.SemaphoreType.DMA((6,)), pltpu.SemaphoreType.DMA((8,)), pltpu.SemaphoreType.DMA((8,)),
           pltpu.SemaphoreType.DMA((2, most)), pltpu.SemaphoreType.DMA((2,))],
        compiler_params=pltpu.CompilerParams(
            collective_id=0, has_side_effects=True, vmem_limit_bytes=60 << 20),
        name="ice",
    )(*fields)


def solution(mesh):
    placed = (
        P(None, None, "gx", "gy"),
        P(None, "gx", "gy"),
        P("gx", "gy"),
        P("gx", "gy"),
        P("gx", "gy"),
        P("gx", "gy"),
    )
    return jax.shard_map(
        per_device, mesh=mesh, in_specs=placed, out_specs=P(None, None, "gx", "gy"), check_vma=False
    )
```

```python
import itertools

import jax
import jax.numpy as jnp
from jax import lax
from jax.experimental import pallas as pl
from jax.experimental.pallas import tpu as pltpu
from jax.sharding import PartitionSpec as P

MESH = pl.DeviceIdType.MESH
F32 = jnp.float32

strain_floor = 0.1
water_drag = 0.25
flow_power = 1.0 / 3.0

GUESS_W, DRAG_W, FLAT_W = 5, 3, 4
MEMBER_LANES = 2 * (GUESS_W + GUESS_W + DRAG_W)
U_AT, V_AT, DRAG_AT = GUESS_W, 3 * GUESS_W, 4 * GUESS_W + DRAG_W
PER_TILE = 4
FLAT_AT = PER_TILE * MEMBER_LANES + FLAT_W
EDGE, HALF = 8, 4
LANES, TILES = 128, 2


def neighbours():
    rows, cols = lax.axis_size("gx"), lax.axis_size("gy")
    me_x, me_y = lax.axis_index("gx"), lax.axis_index("gy")
    up, down = lax.rem(me_x + rows - 1, rows), lax.rem(me_x + 1, rows)
    left, right = lax.rem(me_y + cols - 1, cols), lax.rem(me_y + 1, cols)
    return me_x, me_y, up, down, left, right


def shift(cells, by, axis):
    return pltpu.roll(cells, by % cells.shape[axis], axis)


def beside(tiles, count):
    lane = lax.broadcasted_iota(jnp.int32, tiles[0].shape, 1)
    ring = len(tiles)
    after = [shift(jnp.where(lane == 0, tiles[(t + 1) % ring], tiles[t]), -1, 1) for t in range(count)]
    before = [shift(jnp.where(lane == LANES - 1, tiles[t - 1], tiles[t]), 1, 1) for t in range(count)]
    return after, before


def diff_cols(tiles, count=3):
    return [ahead - behind for ahead, behind in zip(*beside(tiles, count))]


def form(a, b, c):
    return a * (a + b) + b * b + c * (0.25 * c)


def row_places():
    guess = [GUESS_W * i for i in range(2 * PER_TILE)]
    drag = [GUESS_W * 2 * PER_TILE + DRAG_W * i for i in range(PER_TILE)]
    flat = GUESS_W * 2 * PER_TILE + DRAG_W * PER_TILE
    return guess, drag, (flat, flat + FLAT_W)


def spread(axes):
    sizes = [size for size, _, _ in axes]
    place = 0
    for size, mine, _ in axes:
        place = place * size + mine
    steps = [step for step in itertools.product(*map(range, sizes)) if any(step)]

    def reach(step):
        return sum(min(by, size - by) * far for by, (size, _, far) in zip(step, axes))

    steps.sort(key=lambda step: -reach(step))
    return place, [[lax.rem(mine + by, size) for by, (size, mine, _) in zip(step, axes)] for step in steps]


def groups():
    rows, cols = lax.axis_size("gx"), lax.axis_size("gy")
    fine = 4 if rows % 4 == 0 else 1
    pair = 2 if cols % 2 == 0 else 1
    me_x, me_y = lax.axis_index("gx"), lax.axis_index("gy")
    place_y, others_y = spread([(cols // pair, me_y // pair, 1.0), (pair, lax.rem(me_y, pair), 0.1)])
    place_x, others_x = spread([(rows // fine, me_x // fine, 1.0), (fine, lax.rem(me_x, fine), 1.0)])
    return [
        (cols, place_y, [(me_x, chip * pair + core) for chip, core in others_y]),
        (rows, place_x, [(deep * fine + wide, me_y) for deep, wide in others_x]),
    ]


def kernel(guess_hbm, fric_hbm, thick_hbm, surf_hbm, ice_hbm, ground_hbm, out_ref,
           guess_ref, fric_ref, thick_ref, surf_ref, ice_ref, ground_ref,
           go_up, go_down, go_left, go_right, in_up, in_down, in_left, in_right,
           guess_ext, drag_ext, thick_ext, surf_ext, strip, z_ref, y_ref,
           push_u, push_v, nu_ref, sxx_ref, sxy_ref, sums_ref, held,
           load_sem, send_sem, recv_sem, push_sem, pull_sem):
    me_x, me_y, up, down, left, right = neighbours()
    around = [(up, me_y), (down, me_y), (me_x, left), (me_x, right),
              (up, left), (up, right), (down, left), (down, right)]
    phases = groups()
    sources = (ice_hbm, ground_hbm, thick_hbm, surf_hbm, guess_hbm, fric_hbm)
    targets = (ice_ref, ground_ref, thick_ref, surf_ref, guess_ref, fric_ref)
    loads = [pltpu.make_async_copy(source, target, load_sem.at[i])
             for i, (source, target) in enumerate(zip(sources, targets))]
    for load in loads:
        load.start()

    barrier = pltpu.get_barrier_semaphore()
    greeted = [place for _, _, others in phases[::-1] for place in others] + around
    for place in greeted:
        pl.semaphore_signal(barrier, inc=1, device_id=place, device_id_type=MESH)

    members, _, rows, cols = guess_ref.shape
    high = rows + 2 * EDGE
    is_top, is_low = me_x == 0, me_x == lax.axis_size("gx") - 1
    is_left, is_right = me_y == 0, me_y == lax.axis_size("gy") - 1
    guess_at, drag_at, flat_at = row_places()

    go_left[...] = jnp.zeros_like(go_left)
    go_right[...] = jnp.zeros_like(go_right)
    for load in loads:
        load.wait()
    ice = ice_ref[...].astype(F32)
    ground = ground_ref[...].astype(F32)
    lane = lax.broadcasted_iota(jnp.int32, (rows, LANES), 1)

    def pack(ext, cells, row_at, width, group, tile, lane_at):
        for t in range(TILES):
            ext[t, EDGE:EDGE + rows, :] = cells[:, t * LANES:(t + 1) * LANES]
        go_up[group, row_at:row_at + width, :] = cells[:width, :]
        go_down[group, row_at:row_at + width, :] = cells[rows - width:, :]
        head = shift(cells[:, :LANES], lane_at, 1)
        tail = shift(cells[:, cols - LANES:], lane_at, 1)
        go_left[tile] = jnp.where((lane >= lane_at) & (lane < lane_at + width), head, go_left[tile])
        go_right[tile] = jnp.where((lane >= lane_at - width) & (lane < lane_at), tail, go_right[tile])

    def every_field(act, group):
        if group == 0:
            act(thick_ext, lambda: ice * thick_ref[...], flat_at[0], FLAT_W, 0, 0, FLAT_AT)
            act(surf_ext, lambda: surf_ref[...], flat_at[1], FLAT_W, 0, 1, FLAT_AT)
        for k in range(PER_TILE):
            m, base = group * PER_TILE + k, k * MEMBER_LANES
            act(guess_ext.at[m, 0], lambda: ice * guess_ref[m, 0], guess_at[2 * k], GUESS_W, group, group, base + U_AT)
            act(guess_ext.at[m, 1], lambda: ice * guess_ref[m, 1], guess_at[2 * k + 1], GUESS_W, group, group, base + V_AT)
            act(drag_ext.at[m], lambda: ice * (ground * fric_ref[m].astype(F32) + water_drag),
                drag_at[k], DRAG_W, group, group, base + DRAG_AT)

    for group in range(2):
        every_field(lambda ext, cells, *where: pack(ext, cells(), *where), group)

    pl.semaphore_wait(barrier, len(greeted))
    above, mid, below = pl.ds(0, EDGE), pl.ds(EDGE, rows), pl.ds(EDGE + rows, EDGE)
    first, final = pl.ds(0, EDGE), pl.ds(rows - EDGE, EDGE)
    late = pl.ds(0, pl.cdiv(flat_at[0], EDGE) * EDGE)
    moves = [
        (0, go_up.at[0], in_down.at[0]),
        (1, go_down.at[0], in_up.at[0]),
        (2, go_left, in_right.at[:, mid]),
        (3, go_right, in_left.at[:, mid]),
        (4, go_left.at[:, first], in_right.at[:, below]),
        (5, go_right.at[:, first], in_left.at[:, below]),
        (6, go_left.at[:, final], in_right.at[:, above]),
        (7, go_right.at[:, final], in_left.at[:, above]),
        (0, go_up.at[1, late], in_down.at[1, late]),
        (1, go_down.at[1, late], in_up.at[1, late]),
    ]
    copies = [
        pltpu.make_async_remote_copy(
            src_ref=source, dst_ref=target, send_sem=send_sem.at[i], recv_sem=recv_sem.at[i],
            device_id=around[place], device_id_type=MESH)
        for i, (place, source, target) in enumerate(moves)
    ]
    for copy in copies:
        copy.start()
    batches = copies[:len(around)], copies[len(around):]
    for copy in batches[0]:
        copy.wait_recv()

    row = lax.broadcasted_iota(jnp.int32, (high, LANES), 0)
    outside = (is_top & (row < EDGE)) | (is_low & (row >= EDGE + rows))
    for tile in range(2):
        west = jnp.where(is_left, 0.0, in_left[tile])
        east = jnp.where(is_right, 0.0, in_right[tile])
        strip[tile] = jnp.where(outside, 0.0, west + east)

    def fill(ext, cells, row_at, width, group, tile, lane_at):
        for t in range(TILES):
            part = slice(t * LANES, (t + 1) * LANES)
            ext[t, EDGE - width:EDGE, :] = jnp.where(is_top, 0.0, in_up[group, row_at:row_at + width, part])
            ext[t, EDGE + rows:EDGE + rows + width, :] = jnp.where(is_low, 0.0, in_down[group, row_at:row_at + width, part])
        ext[TILES] = shift(strip[tile], -lane_at, 1)

    every_field(fill, 0)

    zero = me_x // lax.axis_size("gx")
    window, start = rows + 2 * HALF, EDGE - HALF + zero

    def part(ref, tile, by=0):
        return ref[tile, pl.ds(start + by, window), :]

    def tiles_of(ref, by=0):
        return [part(ref, t, by) for t in range(TILES + 1)]

    def diff_rows(ref):
        return [part(ref, t, 1) - part(ref, t, -1) for t in range(TILES + 1)]

    def keep(ref, tiles):
        for t, tile in enumerate(tiles):
            ref[t, pl.ds(start, window), :] = tile

    thick = tiles_of(thick_ext)
    keep(push_u, [0.5 * h * d for h, d in zip(thick, diff_rows(surf_ext))])
    keep(push_v, [0.5 * h * d for h, d in zip(thick, diff_cols(tiles_of(surf_ext)))])

    def strains(u_ref, v_ref):
        u, v = tiles_of(u_ref), tiles_of(v_ref)
        c = [p + q for p, q in zip(diff_cols(u), diff_rows(v_ref))]
        return u, v, diff_rows(u_ref), diff_cols(v), c

    def operate(nu, drag, u, v, a, b, c):
        sxx, syy, sxy = [], [], []
        for n, p, q, w in zip(nu, a, b, c):
            half, both = 0.5 * n, p + q
            sxx.append(half * (p + both))
            syy.append(half * (q + both))
            sxy.append((0.5 * half) * w)
        keep(sxx_ref, sxx)
        keep(sxy_ref, sxy)
        image_u = [d * p - x - y for d, p, x, y in zip(drag, u, diff_rows(sxx_ref), diff_cols(sxy))]
        image_v = [d * p - x - y for d, p, x, y in zip(drag, v, diff_cols(syy), diff_rows(sxy_ref))]
        return image_u, image_v

    own_row = lax.broadcasted_iota(jnp.int32, (window, LANES), 0)
    own_row = (own_row >= HALF) & (own_row < HALF + rows)

    def member(m, carry):
        thick = tiles_of(thick_ext)
        drag = tiles_of(drag_ext.at[m])
        u, v, a, b, c = strains(guess_ext.at[m, 0], guess_ext.at[m, 1])
        nu = [(0.5 * h) * jnp.exp(-flow_power * jnp.log(0.25 * form(p, q, w) + strain_floor))
              for h, p, q, w in zip(thick, a, b, c)]
        keep(nu_ref, nu)
        near_rows = [part(nu_ref, t, 1) + part(nu_ref, t, -1) for t in range(TILES + 1)]
        near_cols = [ahead + behind for ahead, behind in zip(*beside(nu, TILES + 1))]
        inv_u = [jnp.where(h > 0.0, 1.0 / (x + 0.25 * y + d), 0.0)
                 for h, x, y, d in zip(thick, near_rows, near_cols, drag)]
        inv_v = [jnp.where(h > 0.0, 1.0 / (y + 0.25 * x + d), 0.0)
                 for h, x, y, d in zip(thick, near_rows, near_cols, drag)]
        image_u, image_v = operate(nu, drag, u, v, a, b, c)
        res_u = [-f - q for f, q in zip(tiles_of(push_u), image_u)]
        res_v = [-f - q for f, q in zip(tiles_of(push_v), image_v)]
        keep(z_ref.at[m, 0], [r * i for r, i in zip(res_u, inv_u)])
        keep(z_ref.at[m, 1], [r * i for r, i in zip(res_v, inv_v)])
        z_u, z_v, a, b, c = strains(z_ref.at[m, 0], z_ref.at[m, 1])
        image_u, image_v = operate(nu, drag, z_u, z_v, a, b, c)
        gap_u = [q - r for q, r in zip(image_u, res_u)]
        gap_v = [q - r for q, r in zip(image_v, res_v)]
        y_u = [g * i for g, i in zip(gap_u, inv_u)]
        y_v = [g * i for g, i in zip(gap_v, inv_v)]
        keep(y_ref.at[m, 0], y_u)
        keep(y_ref.at[m, 1], y_v)

        def own(ref, tile, by=0):
            return ref[tile, pl.ds(EDGE + zero + by, rows), :]

        across_u = diff_cols([own(y_ref.at[m, 0], t) for t in range(TILES + 1)], TILES)
        across_v = diff_cols([own(y_ref.at[m, 1], t) for t in range(TILES + 1)], TILES)
        energy = []
        for t in range(TILES):
            pu, pv = own(y_ref.at[m, 0], t), own(y_ref.at[m, 1], t)
            a = own(y_ref.at[m, 0], t, 1) - own(y_ref.at[m, 0], t, -1)
            c = across_u[t] + own(y_ref.at[m, 1], t, 1) - own(y_ref.at[m, 1], t, -1)
            energy.append(own(nu_ref, t) * form(a, across_v[t], c) + own(drag_ext.at[m], t) * (pu * pu + pv * pv))

        def dot(fu, fv, gu, gv):
            return [jnp.where(own_row, fu[t] * gu[t] + fv[t] * gv[t], 0.0) for t in range(TILES)]

        for i, cells in enumerate((dot(res_u, res_v, z_u, z_v), dot(res_u, res_v, y_u, y_v),
                                   dot(gap_u, gap_v, y_u, y_v), energy)):
            sums_ref[pl.ds(i * members + m, 1), :] = jnp.sum(sum(cells[1:], cells[0]), axis=0, keepdims=True)
        return carry

    for group in range(2):
        if group:
            for copy in batches[group]:
                copy.wait_recv()
            every_field(fill, group)
        lax.fori_loop(group * PER_TILE, (group + 1) * PER_TILE, member, 0, unroll=PER_TILE)
    sums = jnp.sum(sums_ref[...], axis=1, keepdims=True)
    slot = lax.broadcasted_iota(jnp.int32, (sums.shape[0], LANES), 0) == lax.broadcasted_iota(
        jnp.int32, (sums.shape[0], LANES), 1)
    total = jnp.sum(jnp.where(slot, sums, 0.0), axis=0, keepdims=True)

    pushes = []
    for phase, (size, me, others) in enumerate(phases):
        slots = held.at[phase]
        slots[me] = total
        batch = [
            pltpu.make_async_remote_copy(
                src_ref=slots.at[me], dst_ref=slots.at[me], send_sem=push_sem.at[phase, i],
                recv_sem=pull_sem.at[phase], device_id=place, device_id_type=MESH)
            for i, place in enumerate(others)
        ]
        for push in batch:
            push.start()
        everything = slots.at[pl.ds(0, size - 1)]
        pltpu.make_async_copy(everything, everything, pull_sem.at[phase]).wait()
        total = slots[0]
        for i in range(1, size):
            total = total + slots[i]
        pushes += batch

    rz, cross, square, energy = (shift(total, -i * members, 1) for i in range(4))
    scale = rz + cross
    alpha = rz / scale
    mixed = cross + square
    eta = mixed / scale
    top = square - cross * cross / rz
    low = energy - mixed * eta
    step_two = jnp.where(low > 0.0, jnp.maximum(top, 0.0) / low, 0.0)
    to_z, to_y = alpha * (1.0 + step_two * eta), -(alpha * step_two)
    for m in range(members):
        by_z, by_y = to_z[:, m:m + 1], to_y[:, m:m + 1]
        for i in range(2):
            for t in range(TILES):
                own = pl.ds(EDGE, rows)
                out_ref[m, i, :, t * LANES:(t + 1) * LANES] = guess_ext[m, i, t, own, :] + (
                    by_z * z_ref[m, i, t, own, :] + by_y * y_ref[m, i, t, own, :])
    for copy in copies + pushes:
        copy.wait_send()


def per_device(velocity_guess, friction, thickness, surface, ice_mask, grounded_mask):
    members, _, rows, cols = velocity_guess.shape
    fields = (velocity_guess, friction, thickness, surface, ice_mask, grounded_mask)
    packed = row_places()[2][1] + FLAT_W
    packed = pl.cdiv(packed, EDGE) * EDGE
    high = rows + 2 * EDGE
    flat = (TILES + 1, high, LANES)
    count_x, count_y = lax.axis_size("gx"), lax.axis_size("gy")
    most = max(count_x, count_y)
    line, block, side = (2, packed, cols), (2, rows, LANES), (2, high, LANES)
    field = (members, 2, rows, cols)
    return pl.pallas_call(
        kernel,
        out_shape=jax.ShapeDtypeStruct(field, F32),
        in_specs=[pl.BlockSpec(memory_space=pltpu.HBM)] * 6,
        out_specs=pl.BlockSpec(memory_space=pltpu.VMEM),
        scratch_shapes=[pltpu.VMEM(array.shape, array.dtype) for array in fields]
        + [pltpu.VMEM(shape, F32) for shape in (
            line, line, block, block, line, line, side, side,
            (members, 2) + flat, (members,) + flat, flat, flat, side,
            (members, 2) + flat, (members, 2) + flat, flat, flat, flat, flat, flat, (4 * members, LANES), (2, most, 1, LANES))]
        + [pltpu.SemaphoreType.DMA((6,)), pltpu.SemaphoreType.DMA((10,)), pltpu.SemaphoreType.DMA((10,)),
           pltpu.SemaphoreType.DMA((2, most)), pltpu.SemaphoreType.DMA((2,))],
        compiler_params=pltpu.CompilerParams(
            collective_id=0, has_side_effects=True, vmem_limit_bytes=60 << 20),
        name="ice",
    )(*fields)


def solution(mesh):
    placed = (
        P(None, None, "gx", "gy"),
        P(None, "gx", "gy"),
        P("gx", "gy"),
        P("gx", "gy"),
        P("gx", "gy"),
        P("gx", "gy"),
    )
    return jax.shard_map(
        per_device, mesh=mesh, in_specs=placed, out_specs=P(None, None, "gx", "gy"), check_vma=False
    )
```

```python
import itertools

import jax
import jax.numpy as jnp
from jax import lax
from jax.experimental import pallas as pl
from jax.experimental.pallas import tpu as pltpu
from jax.sharding import PartitionSpec as P

MESH = pl.DeviceIdType.MESH
F32 = jnp.float32

strain_floor = 0.1
water_drag = 0.25
flow_power = 1.0 / 3.0

GUESS_W, DRAG_W, FLAT_W = 5, 3, 4
MEMBER_LANES = 2 * (GUESS_W + GUESS_W + DRAG_W)
U_AT, V_AT, DRAG_AT = GUESS_W, 3 * GUESS_W, 4 * GUESS_W + DRAG_W
PER_TILE = 4
FLAT_AT = PER_TILE * MEMBER_LANES + FLAT_W
EDGE, HALF = 8, 4
LANES, TILES = 128, 2


def neighbours():
    rows, cols = lax.axis_size("gx"), lax.axis_size("gy")
    me_x, me_y = lax.axis_index("gx"), lax.axis_index("gy")
    up, down = lax.rem(me_x + rows - 1, rows), lax.rem(me_x + 1, rows)
    left, right = lax.rem(me_y + cols - 1, cols), lax.rem(me_y + 1, cols)
    return me_x, me_y, up, down, left, right


def shift(cells, by, axis):
    return pltpu.roll(cells, by % cells.shape[axis], axis)


def beside(tiles, count):
    lane = lax.broadcasted_iota(jnp.int32, tiles[0].shape, 1)
    ring = len(tiles)
    after = [shift(jnp.where(lane == 0, tiles[(t + 1) % ring], tiles[t]), -1, 1) for t in range(count)]
    before = [shift(jnp.where(lane == LANES - 1, tiles[t - 1], tiles[t]), 1, 1) for t in range(count)]
    return after, before


def diff_cols(tiles, count=3):
    return [ahead - behind for ahead, behind in zip(*beside(tiles, count))]


def form(a, b, c):
    return a * (a + b) + b * b + c * (0.25 * c)


def row_places():
    guess = [GUESS_W * i for i in range(2 * PER_TILE)]
    drag = [GUESS_W * 2 * PER_TILE + DRAG_W * i for i in range(PER_TILE)]
    flat = GUESS_W * 2 * PER_TILE + DRAG_W * PER_TILE
    return guess, drag, (flat, flat + FLAT_W)


def spread(axes):
    sizes = [size for size, _, _ in axes]
    place = 0
    for size, mine, _ in axes:
        place = place * size + mine
    steps = [step for step in itertools.product(*map(range, sizes)) if any(step)]

    def reach(step):
        return sum(min(by, size - by) * far for by, (size, _, far) in zip(step, axes))

    steps.sort(key=lambda step: -reach(step))
    return place, [[lax.rem(mine + by, size) for by, (size, mine, _) in zip(step, axes)] for step in steps]


def groups():
    rows, cols = lax.axis_size("gx"), lax.axis_size("gy")
    fine = 4 if rows % 4 == 0 else 1
    pair = 2 if cols % 2 == 0 else 1
    me_x, me_y = lax.axis_index("gx"), lax.axis_index("gy")
    wide, deep, tall, core = lax.rem(me_x, fine), me_x // fine, me_y // pair, lax.rem(me_y, pair)
    place_z, others_z = spread([(rows // fine, deep, 1.0), (pair, core, 0.1)])
    place_y, others_y = spread([(cols // pair, tall, 1.0), (fine, wide, 1.0)])
    return [
        (rows // fine * pair, place_z, [(d * fine + wide, tall * pair + c) for d, c in others_z]),
        (cols // pair * fine, place_y, [(deep * fine + w, t * pair + core) for t, w in others_y]),
    ]


def kernel(guess_hbm, fric_hbm, thick_hbm, surf_hbm, ice_hbm, ground_hbm, out_ref,
           guess_ref, fric_ref, thick_ref, surf_ref, ice_ref, ground_ref,
           go_up, go_down, go_left, go_right, in_up, in_down, in_left, in_right,
           guess_ext, drag_ext, thick_ext, surf_ext, strip, z_ref, y_ref,
           push_u, push_v, nu_ref, sxx_ref, sxy_ref, sums_ref, held,
           load_sem, send_sem, recv_sem, push_sem, pull_sem):
    me_x, me_y, up, down, left, right = neighbours()
    around = [(up, me_y), (down, me_y), (me_x, left), (me_x, right),
              (up, left), (up, right), (down, left), (down, right)]
    phases = groups()
    sources = (ice_hbm, ground_hbm, thick_hbm, surf_hbm, guess_hbm, fric_hbm)
    targets = (ice_ref, ground_ref, thick_ref, surf_ref, guess_ref, fric_ref)
    loads = [pltpu.make_async_copy(source, target, load_sem.at[i])
             for i, (source, target) in enumerate(zip(sources, targets))]
    for load in loads:
        load.start()

    barrier = pltpu.get_barrier_semaphore()
    greeted = [place for _, _, others in phases[::-1] for place in others] + around
    for place in greeted:
        pl.semaphore_signal(barrier, inc=1, device_id=place, device_id_type=MESH)

    members, _, rows, cols = guess_ref.shape
    high = rows + 2 * EDGE
    is_top, is_low = me_x == 0, me_x == lax.axis_size("gx") - 1
    is_left, is_right = me_y == 0, me_y == lax.axis_size("gy") - 1
    guess_at, drag_at, flat_at = row_places()

    go_left[...] = jnp.zeros_like(go_left)
    go_right[...] = jnp.zeros_like(go_right)
    for load in loads:
        load.wait()
    ice = ice_ref[...].astype(F32)
    ground = ground_ref[...].astype(F32)
    lane = lax.broadcasted_iota(jnp.int32, (rows, LANES), 1)

    def pack(ext, cells, row_at, width, group, tile, lane_at):
        for t in range(TILES):
            ext[t, EDGE:EDGE + rows, :] = cells[:, t * LANES:(t + 1) * LANES]
        go_up[group, row_at:row_at + width, :] = cells[:width, :]
        go_down[group, row_at:row_at + width, :] = cells[rows - width:, :]
        head = shift(cells[:, :LANES], lane_at, 1)
        tail = shift(cells[:, cols - LANES:], lane_at, 1)
        go_left[tile] = jnp.where((lane >= lane_at) & (lane < lane_at + width), head, go_left[tile])
        go_right[tile] = jnp.where((lane >= lane_at - width) & (lane < lane_at), tail, go_right[tile])

    def every_field(act, group):
        if group == 0:
            act(thick_ext, lambda: ice * thick_ref[...], flat_at[0], FLAT_W, 0, 0, FLAT_AT)
            act(surf_ext, lambda: surf_ref[...], flat_at[1], FLAT_W, 0, 1, FLAT_AT)
        for k in range(PER_TILE):
            m, base = group * PER_TILE + k, k * MEMBER_LANES
            act(guess_ext.at[m, 0], lambda: ice * guess_ref[m, 0], guess_at[2 * k], GUESS_W, group, group, base + U_AT)
            act(guess_ext.at[m, 1], lambda: ice * guess_ref[m, 1], guess_at[2 * k + 1], GUESS_W, group, group, base + V_AT)
            act(drag_ext.at[m], lambda: ice * (ground * fric_ref[m].astype(F32) + water_drag),
                drag_at[k], DRAG_W, group, group, base + DRAG_AT)

    for group in range(2):
        every_field(lambda ext, cells, *where: pack(ext, cells(), *where), group)

    pl.semaphore_wait(barrier, len(greeted))
    above, mid, below = pl.ds(0, EDGE), pl.ds(EDGE, rows), pl.ds(EDGE + rows, EDGE)
    first, final = pl.ds(0, EDGE), pl.ds(rows - EDGE, EDGE)
    late = pl.ds(0, pl.cdiv(flat_at[0], EDGE) * EDGE)
    moves = [
        (0, go_up.at[0], in_down.at[0]),
        (1, go_down.at[0], in_up.at[0]),
        (2, go_left, in_right.at[:, mid]),
        (3, go_right, in_left.at[:, mid]),
        (4, go_left.at[:, first], in_right.at[:, below]),
        (5, go_right.at[:, first], in_left.at[:, below]),
        (6, go_left.at[:, final], in_right.at[:, above]),
        (7, go_right.at[:, final], in_left.at[:, above]),
        (0, go_up.at[1, late], in_down.at[1, late]),
        (1, go_down.at[1, late], in_up.at[1, late]),
    ]
    copies = [
        pltpu.make_async_remote_copy(
            src_ref=source, dst_ref=target, send_sem=send_sem.at[i], recv_sem=recv_sem.at[i],
            device_id=around[place], device_id_type=MESH)
        for i, (place, source, target) in enumerate(moves)
    ]
    for copy in copies:
        copy.start()
    batches = copies[:len(around)], copies[len(around):]
    for copy in batches[0]:
        copy.wait_recv()

    row = lax.broadcasted_iota(jnp.int32, (high, LANES), 0)
    outside = (is_top & (row < EDGE)) | (is_low & (row >= EDGE + rows))
    for tile in range(2):
        west = jnp.where(is_left, 0.0, in_left[tile])
        east = jnp.where(is_right, 0.0, in_right[tile])
        strip[tile] = jnp.where(outside, 0.0, west + east)

    def fill(ext, cells, row_at, width, group, tile, lane_at):
        for t in range(TILES):
            part = slice(t * LANES, (t + 1) * LANES)
            ext[t, EDGE - width:EDGE, :] = jnp.where(is_top, 0.0, in_up[group, row_at:row_at + width, part])
            ext[t, EDGE + rows:EDGE + rows + width, :] = jnp.where(is_low, 0.0, in_down[group, row_at:row_at + width, part])
        ext[TILES] = shift(strip[tile], -lane_at, 1)

    every_field(fill, 0)

    zero = me_x // lax.axis_size("gx")
    window, start = rows + 2 * HALF, EDGE - HALF + zero

    def part(ref, tile, by=0):
        return ref[tile, pl.ds(start + by, window), :]

    def tiles_of(ref, by=0):
        return [part(ref, t, by) for t in range(TILES + 1)]

    def diff_rows(ref):
        return [part(ref, t, 1) - part(ref, t, -1) for t in range(TILES + 1)]

    def keep(ref, tiles):
        for t, tile in enumerate(tiles):
            ref[t, pl.ds(start, window), :] = tile

    thick = tiles_of(thick_ext)
    keep(push_u, [0.5 * h * d for h, d in zip(thick, diff_rows(surf_ext))])
    keep(push_v, [0.5 * h * d for h, d in zip(thick, diff_cols(tiles_of(surf_ext)))])

    def strains(u_ref, v_ref):
        u, v = tiles_of(u_ref), tiles_of(v_ref)
        c = [p + q for p, q in zip(diff_cols(u), diff_rows(v_ref))]
        return u, v, diff_rows(u_ref), diff_cols(v), c

    def operate(nu, drag, u, v, a, b, c):
        sxx, syy, sxy = [], [], []
        for n, p, q, w in zip(nu, a, b, c):
            half, both = 0.5 * n, p + q
            sxx.append(half * (p + both))
            syy.append(half * (q + both))
            sxy.append((0.5 * half) * w)
        keep(sxx_ref, sxx)
        keep(sxy_ref, sxy)
        image_u = [d * p - x - y for d, p, x, y in zip(drag, u, diff_rows(sxx_ref), diff_cols(sxy))]
        image_v = [d * p - x - y for d, p, x, y in zip(drag, v, diff_cols(syy), diff_rows(sxy_ref))]
        return image_u, image_v

    own_row = lax.broadcasted_iota(jnp.int32, (window, LANES), 0)
    own_row = (own_row >= HALF) & (own_row < HALF + rows)

    def member(m, carry):
        thick = tiles_of(thick_ext)
        drag = tiles_of(drag_ext.at[m])
        u, v, a, b, c = strains(guess_ext.at[m, 0], guess_ext.at[m, 1])
        nu = [(0.5 * h) * jnp.exp(-flow_power * jnp.log(0.25 * form(p, q, w) + strain_floor))
              for h, p, q, w in zip(thick, a, b, c)]
        keep(nu_ref, nu)
        near_rows = [part(nu_ref, t, 1) + part(nu_ref, t, -1) for t in range(TILES + 1)]
        near_cols = [ahead + behind for ahead, behind in zip(*beside(nu, TILES + 1))]
        inv_u = [jnp.where(h > 0.0, 1.0 / (x + 0.25 * y + d), 0.0)
                 for h, x, y, d in zip(thick, near_rows, near_cols, drag)]
        inv_v = [jnp.where(h > 0.0, 1.0 / (y + 0.25 * x + d), 0.0)
                 for h, x, y, d in zip(thick, near_rows, near_cols, drag)]
        image_u, image_v = operate(nu, drag, u, v, a, b, c)
        res_u = [-f - q for f, q in zip(tiles_of(push_u), image_u)]
        res_v = [-f - q for f, q in zip(tiles_of(push_v), image_v)]
        keep(z_ref.at[m, 0], [r * i for r, i in zip(res_u, inv_u)])
        keep(z_ref.at[m, 1], [r * i for r, i in zip(res_v, inv_v)])
        z_u, z_v, a, b, c = strains(z_ref.at[m, 0], z_ref.at[m, 1])
        image_u, image_v = operate(nu, drag, z_u, z_v, a, b, c)
        gap_u = [q - r for q, r in zip(image_u, res_u)]
        gap_v = [q - r for q, r in zip(image_v, res_v)]
        y_u = [g * i for g, i in zip(gap_u, inv_u)]
        y_v = [g * i for g, i in zip(gap_v, inv_v)]
        keep(y_ref.at[m, 0], y_u)
        keep(y_ref.at[m, 1], y_v)

        def own(ref, tile, by=0):
            return ref[tile, pl.ds(EDGE + zero + by, rows), :]

        across_u = diff_cols([own(y_ref.at[m, 0], t) for t in range(TILES + 1)], TILES)
        across_v = diff_cols([own(y_ref.at[m, 1], t) for t in range(TILES + 1)], TILES)
        energy = []
        for t in range(TILES):
            pu, pv = own(y_ref.at[m, 0], t), own(y_ref.at[m, 1], t)
            a = own(y_ref.at[m, 0], t, 1) - own(y_ref.at[m, 0], t, -1)
            c = across_u[t] + own(y_ref.at[m, 1], t, 1) - own(y_ref.at[m, 1], t, -1)
            energy.append(own(nu_ref, t) * form(a, across_v[t], c) + own(drag_ext.at[m], t) * (pu * pu + pv * pv))

        def dot(fu, fv, gu, gv):
            return [jnp.where(own_row, fu[t] * gu[t] + fv[t] * gv[t], 0.0) for t in range(TILES)]

        for i, cells in enumerate((dot(res_u, res_v, z_u, z_v), dot(res_u, res_v, y_u, y_v),
                                   dot(gap_u, gap_v, y_u, y_v), energy)):
            sums_ref[pl.ds(i * members + m, 1), :] = jnp.sum(sum(cells[1:], cells[0]), axis=0, keepdims=True)
        return carry

    for group in range(2):
        if group:
            for copy in batches[group]:
                copy.wait_recv()
            every_field(fill, group)
        lax.fori_loop(group * PER_TILE, (group + 1) * PER_TILE, member, 0, unroll=PER_TILE)
    sums = jnp.sum(sums_ref[...], axis=1, keepdims=True)
    slot = lax.broadcasted_iota(jnp.int32, (sums.shape[0], LANES), 0) == lax.broadcasted_iota(
        jnp.int32, (sums.shape[0], LANES), 1)
    total = jnp.sum(jnp.where(slot, sums, 0.0), axis=0, keepdims=True)

    for phase, (size, me, others) in enumerate(phases):
        slots = held.at[phase]
        slots[me] = total
        batch = [
            pltpu.make_async_remote_copy(
                src_ref=slots.at[me], dst_ref=slots.at[me], send_sem=push_sem.at[phase],
                recv_sem=pull_sem.at[phase], device_id=place, device_id_type=MESH)
            for place in others
        ]
        for push in batch:
            push.start()
        everything = slots.at[pl.ds(0, size - 1)]
        if phase == 0:
            for copy in copies:
                copy.wait_send()
        pltpu.make_async_copy(everything, everything, push_sem.at[phase]).wait()
        pltpu.make_async_copy(everything, everything, pull_sem.at[phase]).wait()
        total = slots[0]
        for i in range(1, size):
            total = total + slots[i]

    rz, cross, square, energy = (shift(total, -i * members, 1) for i in range(4))
    scale = rz + cross
    alpha = rz / scale
    mixed = cross + square
    eta = mixed / scale
    top = square - cross * cross / rz
    low = energy - mixed * eta
    step_two = jnp.where(low > 0.0, jnp.maximum(top, 0.0) / low, 0.0)
    to_z, to_y = alpha * (1.0 + step_two * eta), -(alpha * step_two)
    for m in range(members):
        by_z, by_y = to_z[:, m:m + 1], to_y[:, m:m + 1]
        for i in range(2):
            for t in range(TILES):
                own = pl.ds(EDGE, rows)
                out_ref[m, i, :, t * LANES:(t + 1) * LANES] = guess_ext[m, i, t, own, :] + (
                    by_z * z_ref[m, i, t, own, :] + by_y * y_ref[m, i, t, own, :])


def per_device(velocity_guess, friction, thickness, surface, ice_mask, grounded_mask):
    members, _, rows, cols = velocity_guess.shape
    fields = (velocity_guess, friction, thickness, surface, ice_mask, grounded_mask)
    packed = row_places()[2][1] + FLAT_W
    packed = pl.cdiv(packed, EDGE) * EDGE
    high = rows + 2 * EDGE
    flat = (TILES + 1, high, LANES)
    count_x, count_y = lax.axis_size("gx"), lax.axis_size("gy")
    most = max(count_x, count_y)
    line, block, side = (2, packed, cols), (2, rows, LANES), (2, high, LANES)
    field = (members, 2, rows, cols)
    return pl.pallas_call(
        kernel,
        out_shape=jax.ShapeDtypeStruct(field, F32),
        in_specs=[pl.BlockSpec(memory_space=pltpu.HBM)] * 6,
        out_specs=pl.BlockSpec(memory_space=pltpu.VMEM),
        scratch_shapes=[pltpu.VMEM(array.shape, array.dtype) for array in fields]
        + [pltpu.VMEM(shape, F32) for shape in (
            line, line, block, block, line, line, side, side,
            (members, 2) + flat, (members,) + flat, flat, flat, side,
            (members, 2) + flat, (members, 2) + flat, flat, flat, flat, flat, flat, (4 * members, LANES), (2, most, 1, LANES))]
        + [pltpu.SemaphoreType.DMA((6,)), pltpu.SemaphoreType.DMA((10,)), pltpu.SemaphoreType.DMA((10,)),
           pltpu.SemaphoreType.DMA((2,)), pltpu.SemaphoreType.DMA((2,))],
        compiler_params=pltpu.CompilerParams(
            collective_id=0, has_side_effects=True, vmem_limit_bytes=60 << 20),
        name="ice",
    )(*fields)


def solution(mesh):
    placed = (
        P(None, None, "gx", "gy"),
        P(None, "gx", "gy"),
        P("gx", "gy"),
        P("gx", "gy"),
        P("gx", "gy"),
        P("gx", "gy"),
    )
    return jax.shard_map(
        per_device, mesh=mesh, in_specs=placed, out_specs=P(None, None, "gx", "gy"), check_vma=False
    )
```

```python
import itertools

import jax
import jax.numpy as jnp
from jax import lax
from jax.experimental import pallas as pl
from jax.experimental.pallas import tpu as pltpu
from jax.sharding import PartitionSpec as P

MESH = pl.DeviceIdType.MESH
F32 = jnp.float32

strain_floor = 0.1
water_drag = 0.25
flow_power = 1.0 / 3.0

GUESS_W, DRAG_W, FLAT_W = 5, 3, 4
MEMBER_LANES = 2 * (GUESS_W + GUESS_W + DRAG_W)
U_AT, V_AT, DRAG_AT = GUESS_W, 3 * GUESS_W, 4 * GUESS_W + DRAG_W
PER_TILE = 4
EARLY = 3
FLAT_AT = PER_TILE * MEMBER_LANES + FLAT_W
EDGE, HALF = 8, 4
LANES, TILES = 128, 2


def neighbours():
    rows, cols = lax.axis_size("gx"), lax.axis_size("gy")
    me_x, me_y = lax.axis_index("gx"), lax.axis_index("gy")
    up, down = lax.rem(me_x + rows - 1, rows), lax.rem(me_x + 1, rows)
    left, right = lax.rem(me_y + cols - 1, cols), lax.rem(me_y + 1, cols)
    return me_x, me_y, up, down, left, right


def shift(cells, by, axis):
    return pltpu.roll(cells, by % cells.shape[axis], axis)


def beside(tiles, count):
    lane = lax.broadcasted_iota(jnp.int32, tiles[0].shape, 1)
    ring = len(tiles)
    after = [shift(jnp.where(lane == 0, tiles[(t + 1) % ring], tiles[t]), -1, 1) for t in range(count)]
    before = [shift(jnp.where(lane == LANES - 1, tiles[t - 1], tiles[t]), 1, 1) for t in range(count)]
    return after, before


def diff_cols(tiles, count=3):
    return [ahead - behind for ahead, behind in zip(*beside(tiles, count))]


def form(a, b, c):
    return a * (a + b) + b * b + c * (0.25 * c)


def row_places(count):
    guess = [GUESS_W * i for i in range(2 * count)]
    drag = [GUESS_W * 2 * count + DRAG_W * i for i in range(count)]
    flat = GUESS_W * 2 * count + DRAG_W * count
    return guess, drag, (flat, flat + FLAT_W), flat + 2 * FLAT_W


def whole_rows(count):
    return pl.cdiv(count, EDGE) * EDGE


def spread(axes):
    sizes = [size for size, _, _ in axes]
    place = 0
    for size, mine, _ in axes:
        place = place * size + mine
    steps = [step for step in itertools.product(*map(range, sizes)) if any(step)]

    def reach(step):
        return sum(min(by, size - by) * far for by, (size, _, far) in zip(step, axes))

    steps.sort(key=lambda step: -reach(step))
    return place, [[lax.rem(mine + by, size) for by, (size, mine, _) in zip(step, axes)] for step in steps]


def groups():
    rows, cols = lax.axis_size("gx"), lax.axis_size("gy")
    fine = 4 if rows % 4 == 0 else 1
    pair = 2 if cols % 2 == 0 else 1
    me_x, me_y = lax.axis_index("gx"), lax.axis_index("gy")
    wide, deep, tall, core = lax.rem(me_x, fine), me_x // fine, me_y // pair, lax.rem(me_y, pair)
    place_z, others_z = spread([(rows // fine, deep, 1.0), (pair, core, 0.1)])
    place_y, others_y = spread([(cols // pair, tall, 1.0), (fine, wide, 1.0)])
    return [
        (rows // fine * pair, place_z, [(d * fine + wide, tall * pair + c) for d, c in others_z]),
        (cols // pair * fine, place_y, [(deep * fine + w, t * pair + core) for t, w in others_y]),
    ]


def kernel(guess_hbm, fric_hbm, thick_hbm, surf_hbm, ice_hbm, ground_hbm, out_ref,
           guess_ref, fric_ref, thick_ref, surf_ref, ice_ref, ground_ref,
           go_up, go_down, go_left, go_right, in_up, in_down, in_left, in_right,
           guess_ext, drag_ext, thick_ext, surf_ext, strip, z_ref, y_ref,
           push_u, push_v, nu_ref, sxx_ref, sxy_ref, sums_ref, held,
           load_sem, send_sem, recv_sem, push_sem, pull_sem):
    me_x, me_y, up, down, left, right = neighbours()
    around = [(up, me_y), (down, me_y), (me_x, left), (me_x, right),
              (up, left), (up, right), (down, left), (down, right)]
    phases = groups()
    sources = (ice_hbm, ground_hbm, thick_hbm, surf_hbm, guess_hbm, fric_hbm)
    targets = (ice_ref, ground_ref, thick_ref, surf_ref, guess_ref, fric_ref)
    loads = [pltpu.make_async_copy(source, target, load_sem.at[i])
             for i, (source, target) in enumerate(zip(sources, targets))]
    barrier = pltpu.get_barrier_semaphore()
    greeted = [place for _, _, others in phases[::-1] for place in others] + around
    for place in greeted:
        pl.semaphore_signal(barrier, inc=1, device_id=place, device_id_type=MESH)
    for load in loads:
        load.start()

    members, _, rows, cols = guess_ref.shape
    high = rows + 2 * EDGE
    is_top, is_low = me_x == 0, me_x == lax.axis_size("gx") - 1
    is_left, is_right = me_y == 0, me_y == lax.axis_size("gy") - 1
    batch_of = (range(0, EARLY), range(EARLY, members))
    placed = [row_places(len(batch)) for batch in batch_of]

    go_left[...] = jnp.zeros_like(go_left)
    go_right[...] = jnp.zeros_like(go_right)
    for load in loads:
        load.wait()
    ice = ice_ref[...].astype(F32)
    ground = ground_ref[...].astype(F32)
    lane = lax.broadcasted_iota(jnp.int32, (rows, LANES), 1)

    def pack(ext, cells, row_at, width, group, tile, lane_at):
        for t in range(TILES):
            ext[t, EDGE:EDGE + rows, :] = cells[:, t * LANES:(t + 1) * LANES]
        go_up[group, row_at:row_at + width, :] = cells[:width, :]
        go_down[group, row_at:row_at + width, :] = cells[rows - width:, :]
        head = shift(cells[:, :LANES], lane_at, 1)
        tail = shift(cells[:, cols - LANES:], lane_at, 1)
        go_left[tile] = jnp.where((lane >= lane_at) & (lane < lane_at + width), head, go_left[tile])
        go_right[tile] = jnp.where((lane >= lane_at - width) & (lane < lane_at), tail, go_right[tile])

    def every_field(act, group):
        if group == 0:
            act(thick_ext, lambda: ice * thick_ref[...], placed[0][2][0], FLAT_W, 0, 0, FLAT_AT)
            act(surf_ext, lambda: surf_ref[...], placed[0][2][1], FLAT_W, 0, 1, FLAT_AT)
        guess_at, drag_at = placed[group][:2]
        for k, m in enumerate(batch_of[group]):
            tile, base = m // PER_TILE, (m % PER_TILE) * MEMBER_LANES
            act(guess_ext.at[m, 0], lambda: ice * guess_ref[m, 0], guess_at[2 * k], GUESS_W, group, tile, base + U_AT)
            act(guess_ext.at[m, 1], lambda: ice * guess_ref[m, 1], guess_at[2 * k + 1], GUESS_W, group, tile, base + V_AT)
            act(drag_ext.at[m], lambda: ice * (ground * fric_ref[m].astype(F32) + water_drag),
                drag_at[k], DRAG_W, group, tile, base + DRAG_AT)

    for group in range(2):
        every_field(lambda ext, cells, *where: pack(ext, cells(), *where), group)

    pl.semaphore_wait(barrier, len(greeted))
    above, mid, below = pl.ds(0, EDGE), pl.ds(EDGE, rows), pl.ds(EDGE + rows, EDGE)
    first, final = pl.ds(0, EDGE), pl.ds(rows - EDGE, EDGE)
    early, late = pl.ds(0, whole_rows(placed[0][3])), pl.ds(0, whole_rows(placed[1][2][0]))
    moves = [
        (0, go_up.at[0, early], in_down.at[0, early]),
        (1, go_down.at[0, early], in_up.at[0, early]),
        (2, go_left, in_right.at[:, mid]),
        (3, go_right, in_left.at[:, mid]),
        (4, go_left.at[:, first], in_right.at[:, below]),
        (5, go_right.at[:, first], in_left.at[:, below]),
        (6, go_left.at[:, final], in_right.at[:, above]),
        (7, go_right.at[:, final], in_left.at[:, above]),
        (0, go_up.at[1, late], in_down.at[1, late]),
        (1, go_down.at[1, late], in_up.at[1, late]),
    ]
    copies = [
        pltpu.make_async_remote_copy(
            src_ref=source, dst_ref=target, send_sem=send_sem.at[i], recv_sem=recv_sem.at[i],
            device_id=around[place], device_id_type=MESH)
        for i, (place, source, target) in enumerate(moves)
    ]
    for copy in copies:
        copy.start()
    batches = copies[:len(around)], copies[len(around):]
    for copy in batches[0]:
        copy.wait_recv()

    row = lax.broadcasted_iota(jnp.int32, (high, LANES), 0)
    outside = (is_top & (row < EDGE)) | (is_low & (row >= EDGE + rows))
    for tile in range(2):
        west = jnp.where(is_left, 0.0, in_left[tile])
        east = jnp.where(is_right, 0.0, in_right[tile])
        strip[tile] = jnp.where(outside, 0.0, west + east)

    def fill(ext, cells, row_at, width, group, tile, lane_at):
        for t in range(TILES):
            part = slice(t * LANES, (t + 1) * LANES)
            ext[t, EDGE - width:EDGE, :] = jnp.where(is_top, 0.0, in_up[group, row_at:row_at + width, part])
            ext[t, EDGE + rows:EDGE + rows + width, :] = jnp.where(is_low, 0.0, in_down[group, row_at:row_at + width, part])
        ext[TILES] = shift(strip[tile], -lane_at, 1)

    every_field(fill, 0)

    zero = me_x // lax.axis_size("gx")
    window, start = rows + 2 * HALF, EDGE - HALF + zero

    def part(ref, tile, by=0):
        return ref[tile, pl.ds(start + by, window), :]

    def tiles_of(ref, by=0):
        return [part(ref, t, by) for t in range(TILES + 1)]

    def diff_rows(ref):
        return [part(ref, t, 1) - part(ref, t, -1) for t in range(TILES + 1)]

    def keep(ref, tiles):
        for t, tile in enumerate(tiles):
            ref[t, pl.ds(start, window), :] = tile

    thick = tiles_of(thick_ext)
    keep(push_u, [0.5 * h * d for h, d in zip(thick, diff_rows(surf_ext))])
    keep(push_v, [0.5 * h * d for h, d in zip(thick, diff_cols(tiles_of(surf_ext)))])

    def strains(u_ref, v_ref):
        u, v = tiles_of(u_ref), tiles_of(v_ref)
        c = [p + q for p, q in zip(diff_cols(u), diff_rows(v_ref))]
        return u, v, diff_rows(u_ref), diff_cols(v), c

    def operate(nu, drag, u, v, a, b, c):
        sxx, syy, sxy = [], [], []
        for n, p, q, w in zip(nu, a, b, c):
            half, both = 0.5 * n, p + q
            sxx.append(half * (p + both))
            syy.append(half * (q + both))
            sxy.append((0.5 * half) * w)
        keep(sxx_ref, sxx)
        keep(sxy_ref, sxy)
        image_u = [d * p - x - y for d, p, x, y in zip(drag, u, diff_rows(sxx_ref), diff_cols(sxy))]
        image_v = [d * p - x - y for d, p, x, y in zip(drag, v, diff_cols(syy), diff_rows(sxy_ref))]
        return image_u, image_v

    own_row = lax.broadcasted_iota(jnp.int32, (window, LANES), 0)
    own_row = (own_row >= HALF) & (own_row < HALF + rows)

    def member(m, carry):
        thick = tiles_of(thick_ext)
        drag = tiles_of(drag_ext.at[m])
        u, v, a, b, c = strains(guess_ext.at[m, 0], guess_ext.at[m, 1])
        nu = [(0.5 * h) * jnp.exp(-flow_power * jnp.log(0.25 * form(p, q, w) + strain_floor))
              for h, p, q, w in zip(thick, a, b, c)]
        keep(nu_ref, nu)
        near_rows = [part(nu_ref, t, 1) + part(nu_ref, t, -1) for t in range(TILES + 1)]
        near_cols = [ahead + behind for ahead, behind in zip(*beside(nu, TILES + 1))]
        inv_u = [jnp.where(h > 0.0, 1.0 / (x + 0.25 * y + d), 0.0)
                 for h, x, y, d in zip(thick, near_rows, near_cols, drag)]
        inv_v = [jnp.where(h > 0.0, 1.0 / (y + 0.25 * x + d), 0.0)
                 for h, x, y, d in zip(thick, near_rows, near_cols, drag)]
        image_u, image_v = operate(nu, drag, u, v, a, b, c)
        res_u = [-f - q for f, q in zip(tiles_of(push_u), image_u)]
        res_v = [-f - q for f, q in zip(tiles_of(push_v), image_v)]
        keep(z_ref.at[m, 0], [r * i for r, i in zip(res_u, inv_u)])
        keep(z_ref.at[m, 1], [r * i for r, i in zip(res_v, inv_v)])
        z_u, z_v, a, b, c = strains(z_ref.at[m, 0], z_ref.at[m, 1])
        image_u, image_v = operate(nu, drag, z_u, z_v, a, b, c)
        gap_u = [q - r for q, r in zip(image_u, res_u)]
        gap_v = [q - r for q, r in zip(image_v, res_v)]
        y_u = [g * i for g, i in zip(gap_u, inv_u)]
        y_v = [g * i for g, i in zip(gap_v, inv_v)]
        keep(y_ref.at[m, 0], y_u)
        keep(y_ref.at[m, 1], y_v)

        def own(ref, tile, by=0):
            return ref[tile, pl.ds(EDGE + zero + by, rows), :]

        across_u = diff_cols([own(y_ref.at[m, 0], t) for t in range(TILES + 1)], TILES)
        across_v = diff_cols([own(y_ref.at[m, 1], t) for t in range(TILES + 1)], TILES)
        energy = []
        for t in range(TILES):
            pu, pv = own(y_ref.at[m, 0], t), own(y_ref.at[m, 1], t)
            a = own(y_ref.at[m, 0], t, 1) - own(y_ref.at[m, 0], t, -1)
            c = across_u[t] + own(y_ref.at[m, 1], t, 1) - own(y_ref.at[m, 1], t, -1)
            energy.append(own(nu_ref, t) * form(a, across_v[t], c) + own(drag_ext.at[m], t) * (pu * pu + pv * pv))

        def dot(fu, fv, gu, gv):
            return [jnp.where(own_row, fu[t] * gu[t] + fv[t] * gv[t], 0.0) for t in range(TILES)]

        for i, cells in enumerate((dot(res_u, res_v, z_u, z_v), dot(res_u, res_v, y_u, y_v),
                                   dot(gap_u, gap_v, y_u, y_v), energy)):
            sums_ref[pl.ds(i * members + m, 1), :] = jnp.sum(sum(cells[1:], cells[0]), axis=0, keepdims=True)
        return carry

    for group in range(2):
        if group:
            for copy in batches[group]:
                copy.wait_recv()
            every_field(fill, group)
        batch = batch_of[group]
        lax.fori_loop(batch.start, batch.stop, member, 0, unroll=len(batch))
    sums = jnp.sum(sums_ref[...], axis=1, keepdims=True)
    slot = lax.broadcasted_iota(jnp.int32, (sums.shape[0], LANES), 0) == lax.broadcasted_iota(
        jnp.int32, (sums.shape[0], LANES), 1)
    total = jnp.sum(jnp.where(slot, sums, 0.0), axis=0, keepdims=True)

    for phase, (size, me, others) in enumerate(phases):
        slots = held.at[phase]
        slots[me] = total
        batch = [
            pltpu.make_async_remote_copy(
                src_ref=slots.at[me], dst_ref=slots.at[me], send_sem=push_sem.at[phase],
                recv_sem=pull_sem.at[phase], device_id=place, device_id_type=MESH)
            for place in others
        ]
        for push in batch:
            push.start()
        everything = slots.at[pl.ds(0, size - 1)]
        if phase == 0:
            for copy in copies:
                copy.wait_send()
        pltpu.make_async_copy(everything, everything, push_sem.at[phase]).wait()
        pltpu.make_async_copy(everything, everything, pull_sem.at[phase]).wait()
        total = slots[0]
        for i in range(1, size):
            total = total + slots[i]

    rz, cross, square, energy = (shift(total, -i * members, 1) for i in range(4))
    scale = rz + cross
    alpha = rz / scale
    mixed = cross + square
    eta = mixed / scale
    top = square - cross * cross / rz
    low = energy - mixed * eta
    step_two = jnp.where(low > 0.0, jnp.maximum(top, 0.0) / low, 0.0)
    to_z, to_y = alpha * (1.0 + step_two * eta), -(alpha * step_two)
    for m in range(members):
        by_z, by_y = to_z[:, m:m + 1], to_y[:, m:m + 1]
        for i in range(2):
            for t in range(TILES):
                own = pl.ds(EDGE, rows)
                out_ref[m, i, :, t * LANES:(t + 1) * LANES] = guess_ext[m, i, t, own, :] + (
                    by_z * z_ref[m, i, t, own, :] + by_y * y_ref[m, i, t, own, :])


def per_device(velocity_guess, friction, thickness, surface, ice_mask, grounded_mask):
    members, _, rows, cols = velocity_guess.shape
    fields = (velocity_guess, friction, thickness, surface, ice_mask, grounded_mask)
    packed = whole_rows(max(row_places(EARLY)[3], row_places(members - EARLY)[2][0]))
    high = rows + 2 * EDGE
    flat = (TILES + 1, high, LANES)
    count_x, count_y = lax.axis_size("gx"), lax.axis_size("gy")
    most = max(count_x, count_y)
    line, block, side = (2, packed, cols), (2, rows, LANES), (2, high, LANES)
    field = (members, 2, rows, cols)
    return pl.pallas_call(
        kernel,
        out_shape=jax.ShapeDtypeStruct(field, F32),
        in_specs=[pl.BlockSpec(memory_space=pltpu.HBM)] * 6,
        out_specs=pl.BlockSpec(memory_space=pltpu.VMEM),
        scratch_shapes=[pltpu.VMEM(array.shape, array.dtype) for array in fields]
        + [pltpu.VMEM(shape, F32) for shape in (
            line, line, block, block, line, line, side, side,
            (members, 2) + flat, (members,) + flat, flat, flat, side,
            (members, 2) + flat, (members, 2) + flat, flat, flat, flat, flat, flat, (4 * members, LANES), (2, most, 1, LANES))]
        + [pltpu.SemaphoreType.DMA((6,)), pltpu.SemaphoreType.DMA((10,)), pltpu.SemaphoreType.DMA((10,)),
           pltpu.SemaphoreType.DMA((2,)), pltpu.SemaphoreType.DMA((2,))],
        compiler_params=pltpu.CompilerParams(
            collective_id=0, has_side_effects=True, vmem_limit_bytes=60 << 20),
        name="ice",
    )(*fields)


def solution(mesh):
    placed = (
        P(None, None, "gx", "gy"),
        P(None, "gx", "gy"),
        P("gx", "gy"),
        P("gx", "gy"),
        P("gx", "gy"),
        P("gx", "gy"),
    )
    return jax.shard_map(
        per_device, mesh=mesh, in_specs=placed, out_specs=P(None, None, "gx", "gy"), check_vma=False
    )
```
